256 devices in a mesh: dp: 16 (over x, z_lo), shard: 16 (over z_hi, y, core).
Axes of the slice: x: 4, y: 4, z: 8 (z_hi: 2, z_lo: 4; z = z_hi * 4 + z_lo), core: 2. Of those that a mesh axis runs over, the one named last changes fastest.
Arguments:
- codes: int32 [16, 5, 8, 64], P('dp', None, None, 'shard'), may hold values from 0 to 262143
- lengths: int32 [16], P('dp'), may hold values from 1 to 5, 48 in all
- hidden: bfloat16 [16, 5, 8, 64, 512], P('dp', None, None, 'shard'), may hold values from -6 to 6
- embed: bfloat16 [18, 512], replicated, may hold values from -1.5 to 1.5
- conv_weight: bfloat16 [512, 27, 512], P('shard'), may hold values from -0.0546875 to 0.0546875
- gain: float32 [512], replicated, may hold values from 0.1 to 1.9
- bias: float32 [512], replicated, may hold values from -3 to 3
- cotangent: bfloat16 [16, 5, 16, 128, 128], P('dp', None, None, 'shard'), may hold values from -6 to 6
Outputs:
- decoded: bfloat16 [16, 5, 16, 128, 128], P('dp', None, None, 'shard')
- grad_hidden: bfloat16 [16, 5, 8, 64, 512], P('dp', None, None, 'shard')
- grad_conv: float32 [512, 27, 512], P('shard')
- grad_embed: float32 [18, 512], replicated
- grad_gain: float32 [512], replicated
- grad_bias: float32 [512], replicated
The draws below stay inside these ranges and needn't reach their ends.
Inputs may be any that keep to these rules, and one draw needn't show every extreme that they name: Frames from lengths[c] on are padding; some clip has all 5 frames valid.
All inputs are finite; a program needn't handle non-finite values. No bound on the sum of `lengths` on one device may be relied on, other than what follows from the above.
Results may differ from the reference program's by a relative error of at most 0.02.
Values may be sent and summed in bfloat16 or wider, within the bound.
A program may use at most 128 MiB of HBM per device.

```python
import math
import jax
import jax.numpy as jnp
import numpy as np
from jax import lax

C = 512
CODE_BITS = 18
GROUPS = 32
FRAMES = 5
ROWS = 8
COLS_DEV = 4
COLS = 64
CLIPS = 16
N_DP = 16
N_SHARD = 16


def with_ends(array, key, least, high):
    index_at = [jax.random.randint(jax.random.fold_in(key, axis), (), 0, length) for axis, length in enumerate(array.shape)]
    main_axis = array.shape.index(max(array.shape))
    next_to = index_at[:main_axis] + [(index_at[main_axis] + 1) % array.shape[main_axis]] + index_at[main_axis + 1:]
    return array.at[tuple(index_at)].set(least).at[tuple(next_to)].set(high)


def shard_levels(key, dims, split, low, top_value):
    loudness = 1.0
    for position, parts in split:
        draws = jax.random.uniform(jax.random.fold_in(jax.random.fold_in(key, 6), position), (parts,), jnp.float32, low / len(split), top_value / len(split))
        loudness = loudness * jnp.repeat(jnp.exp(draws), dims[position] // parts).reshape((-1,) + (1,) * (len(dims) - 1 - position))
    return loudness


def profile(count, total, reach, slope):
    loads = [(1 << 20) // math.isqrt(rank ** slope) + 1 for rank in range(2, count + 1)]
    spare, given = total - reach - (count - 1), [1] * (count - 1)
    while spare > 0:
        free = [i for i in range(count - 1) if given[i] < reach]
        mass, left = sum([loads[i] for i in free]), spare
        for i in free:
            more = min(reach - given[i], max(1, left * loads[i] // mass), spare)
            given[i] = given[i] + more
            spare = spare - more
    return np.array([reach] + given)


def ragged_sizes(stream_key, count, total, limit, slope):
    if count == 2:
        one = jax.random.randint(stream_key, (), max(1, total - limit), min(limit, total - 1) + 1)
        return jnp.stack([one, total - one])
    tallies = jnp.asarray(profile(count, total, limit, slope), jnp.int32)
    couples = (count - 1) // 2
    giver, sink = tallies[1:1 + 2 * couples:2], tallies[2:2 + 2 * couples:2]
    room = jnp.minimum(giver - 1, limit - sink)
    moved = jax.random.randint(jax.random.fold_in(stream_key, 1), (couples,), 0, 1 << 20) % (room + 1)
    tallies = tallies.at[1:1 + 2 * couples:2].set(giver - moved).at[2:2 + 2 * couples:2].set(sink + moved)
    return tallies[jax.random.permutation(jax.random.fold_in(stream_key, 2), count)]


def normal_values(own_key, shape, scale, most, split=(), held_as=jnp.bfloat16):
    level = shard_levels(own_key, shape, split, -0.22, 0.18) if split else 1.0
    drawn = jax.random.normal(own_key, shape, jnp.float32) * scale * level
    return jnp.minimum(jnp.maximum(drawn, -most), most).astype(held_as)


def setup_inputs(seed: int = 0) -> dict:
    streams_of = jax.random.split(jax.random.key(seed), 9)
    return {
        "codes": with_ends(jax.random.randint(streams_of[0], (CLIPS, FRAMES, ROWS, COLS), 0, 262144), jax.random.fold_in(streams_of[0], 1), 0, 262143).astype(jnp.int32),
        "lengths": ragged_sizes(streams_of[1], CLIPS, 3 * N_DP, FRAMES, 0).astype(jnp.int32),
        "hidden": normal_values(streams_of[2], (CLIPS, FRAMES, ROWS, COLS, C), 1.0, 6.0, ((0, 16), (3, 16))),
        "embed": normal_values(streams_of[3], (CODE_BITS, C), CODE_BITS ** -0.5, 1.5),
        "conv_weight": normal_values(streams_of[4], (C, 27, C), (27 * C) ** -0.5, 0.0546875, ((0, 16),)),
        "gain": jnp.clip(1.0 + 0.18 * jax.random.normal(streams_of[5], (C,), jnp.float32), 0.1, 1.9),
        "bias": normal_values(streams_of[6], (C,), 0.5, 3.0, (), jnp.float32),
        "cotangent": normal_values(streams_of[7], (CLIPS, FRAMES, 2 * ROWS, 2 * COLS, C // 4), 1.0, 6.0, ((0, 16), (3, 16))),
    }


def front_patches(padded, frames, height, width):
    taps = []
    for depth_tap in range(3):
        for row_tap in range(3):
            for col_tap in range(3):
                taps.append(padded[depth_tap:depth_tap + frames, row_tap:row_tap + height, col_tap:col_tap + width])
    return jnp.stack(taps, axis=3)

def back_patches(padded, frames, height, width):
    taps = []
    for depth_tap in range(3):
        for row_tap in range(3):
            for col_tap in range(3):
                taps.append(padded[2 - depth_tap:2 - depth_tap + frames, 2 - row_tap:2 - row_tap + height, 2 - col_tap:2 - col_tap + width])
    return jnp.stack(taps, axis=3)

def reference(codes, lengths, hidden, embed, conv_weight, gain, bias, cotangent):
    per_group = C // GROUPS
    quarter = C // 4
    columns = COLS_DEV * N_SHARD
    positions = FRAMES * ROWS * columns
    powers = 2 ** jnp.arange(CODE_BITS, dtype=jnp.int32)
    flat_weight = jnp.transpose(conv_weight, (1, 0, 2)).reshape(27 * C, C)
    back_weight = jnp.transpose(conv_weight, (1, 2, 0)).reshape(27 * C, C)
    gain_group = gain.reshape(GROUPS, per_group)
    bias_group = bias.reshape(GROUPS, per_group)

    def one_clip(carry, inputs):
        total_conv, total_embed, total_gain, total_bias = carry
        clip_codes, clip_length, clip_hidden, clip_cot = inputs
        frame_mask = (jnp.arange(FRAMES) < clip_length).astype(jnp.float32)
        mask_cells = frame_mask[:, None, None, None]
        mask_groups = frame_mask[:, None, None, None, None]
        bits = (clip_codes[..., None] // powers % 2 * 2 - 1).astype(jnp.bfloat16)
        embedded = jnp.dot(bits.reshape(positions, CODE_BITS), embed, preferred_element_type=jnp.float32).reshape(FRAMES, ROWS, columns, C)
        features = ((embedded + clip_hidden.astype(jnp.float32)) * mask_cells).astype(jnp.bfloat16)
        padded = jnp.pad(features, ((2, 0), (1, 1), (1, 1), (0, 0)))
        patches = front_patches(padded, FRAMES, ROWS, columns).reshape(positions, 27 * C)
        conv_out = jnp.dot(patches, flat_weight, preferred_element_type=jnp.float32)
        grouped = conv_out.reshape(FRAMES, ROWS, columns, GROUPS, per_group)
        count = clip_length.astype(jnp.float32) * (ROWS * columns * per_group)
        mean = lax.optimization_barrier(jnp.sum(grouped * mask_groups, axis=(0, 1, 2, 4))) / count
        variance = lax.optimization_barrier(jnp.sum(grouped * grouped * mask_groups, axis=(0, 1, 2, 4))) / count - mean * mean
        inv_std = lax.rsqrt(variance + 1e-05)
        normed = (grouped - mean[:, None]) * inv_std[:, None]
        pre = normed * gain_group + bias_group
        sigma = jax.nn.sigmoid(pre)
        activated = pre * sigma * mask_groups
        decoded = activated.reshape(FRAMES, ROWS, columns, 2, 2, quarter).transpose(0, 1, 3, 2, 4, 5).reshape(FRAMES, 2 * ROWS, 2 * columns, quarter).astype(jnp.bfloat16)
        upstream = clip_cot.astype(jnp.float32).reshape(FRAMES, ROWS, 2, columns, 2, quarter).transpose(0, 1, 3, 2, 4, 5).reshape(FRAMES, ROWS, columns, GROUPS, per_group) * mask_groups
        d_pre = upstream * sigma * (1.0 + pre * (1.0 - sigma))
        gain_term = lax.optimization_barrier(jnp.sum(d_pre * normed, axis=(0, 1, 2))).reshape(C)
        bias_term = lax.optimization_barrier(jnp.sum(d_pre, axis=(0, 1, 2))).reshape(C)
        d_norm = d_pre * gain_group
        tot_one = lax.optimization_barrier(jnp.sum(d_norm, axis=(0, 1, 2, 4)))
        tot_two = lax.optimization_barrier(jnp.sum(d_norm * normed, axis=(0, 1, 2, 4)))
        d_conv = (inv_std[:, None] * (d_norm - tot_one[:, None] / count - normed * tot_two[:, None] / count) * mask_groups).reshape(FRAMES, ROWS, columns, C).astype(jnp.bfloat16)
        grad_padded = jnp.pad(d_conv, ((0, 2), (1, 1), (1, 1), (0, 0)))
        grad_patches = back_patches(grad_padded, FRAMES, ROWS, columns)
        d_features = jnp.dot(grad_patches.reshape(positions, 27 * C), back_weight, preferred_element_type=jnp.float32).astype(jnp.bfloat16).reshape(FRAMES, ROWS, columns, C)
        d_features = d_features * mask_cells.astype(jnp.bfloat16)
        embed_term = jnp.dot(bits.reshape(positions, CODE_BITS).T, d_features.reshape(positions, C), preferred_element_type=jnp.float32)
        clip_sum = jnp.dot(patches.T, d_conv.reshape(positions, C), preferred_element_type=jnp.float32)
        clip_sum = lax.optimization_barrier(clip_sum.astype(jnp.bfloat16)).astype(jnp.float32)
        return ((total_conv + clip_sum, total_embed + embed_term, total_gain + gain_term, total_bias + bias_term), (decoded, d_features))
    init = (jnp.zeros((27 * C, C), jnp.float32), jnp.zeros((CODE_BITS, C), jnp.float32), jnp.zeros((C,), jnp.float32), jnp.zeros((C,), jnp.float32))
    totals, outputs = lax.scan(one_clip, init, (codes, lengths, hidden, cotangent))
    decoded, grad_hidden = outputs
    grad_conv = totals[0].reshape(27, C, C).transpose(1, 0, 2)
    return (decoded, grad_hidden, grad_conv, totals[1], totals[2], totals[3])
```

```python
import jax
import jax.numpy as jnp
from jax import lax
from jax.experimental import pallas as pl
from jax.experimental.pallas import tpu as pltpu
from jax.sharding import PartitionSpec as P

BF = jnp.bfloat16
F32 = jnp.float32
CODE_BITS = 18
EPS = 1e-05
T = 5
R = 8
WD = 4
NS = 16
LP = 512
G = 7
MESH = pl.DeviceIdType.MESH
VM = pl.BlockSpec(memory_space=pltpu.VMEM)


def params(cid=None):
    if cid is None:
        return pltpu.CompilerParams(vmem_limit_bytes=60 * 1024 * 1024)
    return pltpu.CompilerParams(
        vmem_limit_bytes=60 * 1024 * 1024, collective_id=cid, has_side_effects=True
    )


def shard_spot():
    me = lax.axis_index("shard")
    return me, me // 8, (me // 2) % 4, me % 2


def sid(z, y, c):
    return z * 8 + y * 2 + c


def barrier(targets):
    sem = pltpu.get_barrier_semaphore()
    for axis, peer in targets:
        pl.semaphore_signal(sem, inc=1, device_id={axis: peer}, device_id_type=MESH)
    pl.semaphore_wait(sem, len(targets))


def rcopy(src, dst, ssem, rsem, axis, peer):
    return pltpu.make_async_remote_copy(
        src_ref=src, dst_ref=dst, send_sem=ssem, recv_sem=rsem,
        device_id={axis: peer}, device_id_type=MESH,
    )


def a2a_body(src, dst, ssem, rsem):
    me = lax.axis_index("shard")
    barrier([("shard", (me + d) % NS) for d in range(1, NS)])
    sends = []
    for d in range(1, NS):
        peer = (me + d) % NS
        cp = rcopy(src.at[peer], dst.at[me], ssem.at[d], rsem.at[d], "shard", peer)
        cp.start()
        sends.append(cp)
    dst[me] = src[me]
    for d in range(1, NS):
        frm = (me + NS - d) % NS
        rcopy(src.at[frm], dst.at[frm], ssem.at[d], rsem.at[d], "shard", frm).wait_recv()
    for cp in sends:
        cp.wait_send()


def exchange_in(blocks):
    return pl.pallas_call(
        a2a_body,
        out_shape=jax.ShapeDtypeStruct(blocks.shape, blocks.dtype),
        in_specs=[VM], out_specs=VM,
        scratch_shapes=[pltpu.SemaphoreType.DMA((NS,)), pltpu.SemaphoreType.DMA((NS,))],
        compiler_params=params(0),
        name="exchange_in",
    )(blocks)


def lane_masks():
    lane = lax.broadcasted_iota(jnp.int32, (1, LP), 1)
    row = (lane // 4) % 8
    col = lane % 4
    return {
        "r0": row >= 1, "r2": row <= 6,
        "c0": col >= 1, "c2": col <= 2,
        "w0": lane % 4 + lane // 32 > 0, "w2": lane % 4 + 4 * (lane // 32) < 63,
    }


def row_shift(x, d, m):
    if d < 0:
        return jnp.where(m["r0"], pltpu.roll(x, 4, 1), 0.0)
    if d > 0:
        return jnp.where(m["r2"], pltpu.roll(x, LP - 4, 1), 0.0)
    return x


def col_shift(x, d, m):
    if d < 0:
        y = jnp.where(m["c0"], pltpu.roll(x, 1, 1), pltpu.roll(x, 29, 1))
        return jnp.where(m["w0"], y, 0.0)
    if d > 0:
        y = jnp.where(m["c2"], pltpu.roll(x, LP - 1, 1), pltpu.roll(x, LP - 29, 1))
        return jnp.where(m["w2"], y, 0.0)
    return x


def dot(a, b):
    return lax.dot_general(a, b, (((1,), (0,)), ((), ())), preferred_element_type=F32)


def dot_nt(a, b):
    return lax.dot_general(a, b, (((1,), (1,)), ((), ())), preferred_element_type=F32)


def forward_body(g_ref, wt_ref, part_ref, ut_ref, bt_ref, pat_ref):
    m = lane_masks()
    eye = (
        lax.broadcasted_iota(jnp.int32, (128, 128), 0)
        == lax.broadcasted_iota(jnp.int32, (128, 128), 1)
    ).astype(F32).astype(BF)
    for t in range(T):
        rows = g_ref[:, t * 32:(t + 1) * 32, :].reshape(LP, 128)
        tt = dot_nt(eye, rows)
        ut_ref[t] = tt[64:96].astype(BF)
        bt_ref[t] = tt[96:128].astype(BF)
        f = tt[0:64]
        for dw in range(3):
            fc = col_shift(f, dw - 1, m)
            for dr in range(3):
                k = 3 * dr + dw
                pat_ref[t, 64 * k:64 * (k + 1), :] = row_shift(fc, dr - 1, m).astype(BF)
    for t in range(T):
        acc = None
        for dt in range(3):
            if t - 2 + dt < 0:
                continue
            d = dot(wt_ref[dt], pat_ref[t - 2 + dt])
            acc = d if acc is None else acc + d
        for k in range(8):
            part_ref[k, t] = acc[32 * k:32 * (k + 1)].astype(BF)


def forward(g, wt):
    return pl.pallas_call(
        forward_body,
        out_shape=(
            jax.ShapeDtypeStruct((8, T, 32, LP), BF),
            jax.ShapeDtypeStruct((T, 32, LP), BF),
            jax.ShapeDtypeStruct((T, 32, LP), BF),
            jax.ShapeDtypeStruct((T, 576, LP), BF),
        ),
        in_specs=[VM, VM], out_specs=(VM,) * 4,
        compiler_params=params(), name="forward",
    )(g, wt)


def scatter_body(p_ref, out_ref, rx1, tx2, rx2, txz, rxz, ssem, rsem):
    me, z, y, c = shard_spot()
    yp, ym = (y + 1) % 4, (y + 3) % 4
    up, down, over = sid(z, yp, c), sid(z, ym, c), sid(1 - z, y, c)
    barrier([("shard", up), ("shard", down), ("shard", over)])
    far = (y + 2) % 4

    def c1(t):
        return (
            rcopy(p_ref.at[:, far, t, pl.ds(0, 16)], rx1.at[0, t], ssem.at[0, t], rsem.at[0, t], "shard", up),
            rcopy(p_ref.at[:, far, t, pl.ds(16, 16)], rx1.at[1, t], ssem.at[1, t], rsem.at[1, t], "shard", down),
        )

    def c2(t):
        return (
            rcopy(tx2.at[0, t], rx2.at[0, t], ssem.at[2, t], rsem.at[2, t], "shard", up),
            rcopy(tx2.at[1, t], rx2.at[1, t], ssem.at[3, t], rsem.at[3, t], "shard", down),
        )

    def c3(t):
        return rcopy(txz.at[t], rxz.at[t], ssem.at[4, t], rsem.at[4, t], "shard", over)

    def s1(t):
        for cp in c1(t):
            cp.start()

    def s2(t):
        a, b = c1(t)
        n, q = c2(t)
        a.wait_recv()
        tx2[0, t, :, 0:16] = (p_ref[:, yp, t, 0:16].astype(F32) + rx1[0, t].astype(F32)).astype(BF)
        tx2[0, t, :, 16:32] = p_ref[:, yp, t, 16:32]
        n.start()
        b.wait_recv()
        tx2[1, t, :, 16:32] = (p_ref[:, ym, t, 16:32].astype(F32) + rx1[1, t].astype(F32)).astype(BF)
        tx2[1, t, :, 0:16] = p_ref[:, ym, t, 0:16]
        q.start()

    def s3(t):
        n, q = c2(t)
        n.wait_recv()
        q.wait_recv()
        txz[t] = (
            p_ref[1 - z, y, t].astype(F32) + rx2[0, t, 1 - z].astype(F32) + rx2[1, t, 1 - z].astype(F32)
        ).astype(BF)
        c3(t).start()
        out_ref[t] = p_ref[z, y, t].astype(F32) + rx2[0, t, z].astype(F32) + rx2[1, t, z].astype(F32)

    def s4(t):
        c3(t).wait_recv()
        out_ref[t] = out_ref[t] + rxz[t].astype(F32)

    stages = (s1, s2, s3, s4)
    for step in range(T + 3):
        for k in range(4):
            t = step - k
            if 0 <= t < T:
                stages[k](t)
    for t in range(T):
        for cp in c1(t) + c2(t) + (c3(t),):
            cp.wait_send()


def scatter(part):
    return pl.pallas_call(
        scatter_body,
        out_shape=jax.ShapeDtypeStruct((T, 32, LP), F32),
        in_specs=[VM], out_specs=VM,
        scratch_shapes=[
            pltpu.VMEM((2, T, 2, 16, LP), BF),
            pltpu.VMEM((2, T, 2, 32, LP), BF),
            pltpu.VMEM((2, T, 2, 32, LP), BF),
            pltpu.VMEM((T, 32, LP), BF),
            pltpu.VMEM((T, 32, LP), BF),
            pltpu.SemaphoreType.DMA((5, T)),
            pltpu.SemaphoreType.DMA((5, T)),
        ],
        compiler_params=params(1), name="scatter",
    )(part)


def group_sum(x):
    s = jnp.sum(x, axis=1, keepdims=True)
    g = jnp.sum(s.reshape(2, 16, 1), axis=1, keepdims=True)
    return jnp.broadcast_to(g, (2, 16, 1)).reshape(32, 1)


def norm_body(len_ref, conv_ref, ut_ref, gain_ref, bias_ref, act_ref, dc_ref, gb_ref, nrm, dpr):
    length = len_ref[0]
    count = length.astype(F32) * (R * WD * NS * 16)
    masks = [jnp.where(t < length, 1.0, 0.0) for t in range(T)]
    s1 = jnp.zeros((32, LP), F32)
    s2 = jnp.zeros((32, LP), F32)
    for t in range(T):
        v = conv_ref[t] * masks[t]
        s1 = s1 + v
        s2 = s2 + conv_ref[t] * v
    mean = group_sum(s1) / count
    var = group_sum(s2) / count - mean * mean
    inv = lax.rsqrt(var + EPS)
    gain = gain_ref[...]
    bias = bias_ref[...]
    a1 = jnp.zeros((32, LP), F32)
    a2 = jnp.zeros((32, LP), F32)
    for t in range(T):
        n = (conv_ref[t] - mean) * inv
        pre = n * gain + bias
        sg = jax.nn.sigmoid(pre)
        act_ref[t] = (pre * sg * masks[t]).astype(BF)
        dp = ut_ref[t].astype(F32) * masks[t] * sg * (1.0 + pre * (1.0 - sg))
        a1 = a1 + dp
        a2 = a2 + dp * n
        nrm[t] = n
        dpr[t] = dp
    bterm = jnp.sum(a1, axis=1, keepdims=True)
    gterm = jnp.sum(a2, axis=1, keepdims=True)
    t1 = group_sum(gain * bterm) / count
    t2 = group_sum(gain * gterm) / count
    for t in range(T):
        dc_ref[t] = (inv * (dpr[t] * gain - t1 - nrm[t] * t2) * masks[t]).astype(BF)
    lane = lax.broadcasted_iota(jnp.int32, (32, 128), 1)
    gb_ref[...] = jnp.where(lane == 0, gterm, jnp.where(lane == 1, bterm, 0.0))


def norm(lengths, conv, ut, gain, bias):
    return pl.pallas_call(
        norm_body,
        out_shape=(
            jax.ShapeDtypeStruct((T, 32, LP), BF),
            jax.ShapeDtypeStruct((T, 32, LP), BF),
            jax.ShapeDtypeStruct((32, 128), F32),
        ),
        in_specs=[pl.BlockSpec(memory_space=pltpu.SMEM), VM, VM, VM, VM],
        out_specs=(VM,) * 3,
        scratch_shapes=[pltpu.VMEM((T, 32, LP), F32), pltpu.VMEM((T, 32, LP), F32)],
        compiler_params=params(), name="norm",
    )(lengths, conv, ut, gain, bias)


def gather_body(own, out, ssem, rsem):
    me, z, y, c = shard_spot()
    o = 1 - z
    yp, ym = (y + 1) % 4, (y + 3) % 4
    up, down, over = sid(z, yp, c), sid(z, ym, c), sid(o, y, c)
    barrier([("shard", up), ("shard", down), ("shard", over)])
    lo, hi = pl.ds(0, 16), pl.ds(16, 16)

    def cp(kind, t, src, dst, peer):
        return rcopy(src, dst, ssem.at[kind, t], rsem.at[kind, t], "shard", peer)

    def send(kind, t):
        if kind == 0:
            return cp(0, t, own.at[t], out.at[z, y, t], over)
        if kind == 1:
            return cp(1, t, own.at[t], out.at[z, y, t], up)
        if kind == 2:
            return cp(2, t, own.at[t], out.at[z, y, t], down)
        if kind == 3:
            return cp(3, t, out.at[z, ym, t, lo], out.at[z, ym, t, lo], up)
        if kind == 4:
            return cp(4, t, out.at[z, yp, t, hi], out.at[z, yp, t, hi], down)
        if kind == 5:
            return cp(5, t, out.at[o, y, t], out.at[o, y, t], up)
        if kind == 6:
            return cp(6, t, out.at[o, y, t], out.at[o, y, t], down)
        if kind == 7:
            return cp(7, t, out.at[o, ym, t, lo], out.at[o, ym, t, lo], up)
        return cp(8, t, out.at[o, yp, t, hi], out.at[o, yp, t, hi], down)

    far = (y + 2) % 4

    def got(kind, t):
        spot = {
            0: (o, y, None), 1: (z, ym, None), 2: (z, yp, None), 3: (z, far, lo), 4: (z, far, hi),
            5: (o, ym, None), 6: (o, yp, None), 7: (o, far, lo), 8: (o, far, hi),
        }[kind]
        ref = out.at[spot[0], spot[1], t] if spot[2] is None else out.at[spot[0], spot[1], t, spot[2]]
        cp(kind, t, ref, ref, over).wait_recv()

    for t in range(T):
        send(0, t).start()
        send(1, t).start()
        send(2, t).start()
    for t in range(T):
        out[z, y, t] = own[t]
    for t in range(T):
        got(1, t)
        send(3, t).start()
        got(2, t)
        send(4, t).start()
    for t in range(T + 1):
        if t < T:
            got(0, t)
            send(5, t).start()
            send(6, t).start()
        if t > 0:
            got(5, t - 1)
            send(7, t - 1).start()
            got(6, t - 1)
            send(8, t - 1).start()
    for t in range(T):
        for kind in (3, 4, 7, 8):
            got(kind, t)
    for t in range(T):
        for kind in range(9):
            send(kind, t).wait_send()


def gather(dconv):
    return pl.pallas_call(
        gather_body,
        out_shape=jax.ShapeDtypeStruct((2, 4, T, 32, LP), BF),
        in_specs=[VM], out_specs=VM,
        scratch_shapes=[pltpu.SemaphoreType.DMA((9, T)), pltpu.SemaphoreType.DMA((9, T))],
        compiler_params=params(2), name="gather",
    )(dconv)


def backward_body(dc_ref, pat_ref, w_ref, cw_ref, df_ref, db_ref):
    m = lane_masks()
    for dt in range(3):
        acc = None
        for t in range(2 - dt, T):
            d = dot_nt(pat_ref[t - 2 + dt], dc_ref[:, t].reshape(256, LP))
            acc = d if acc is None else acc + d
        for k in range(9):
            cw_ref[9 * dt + k] = acc[64 * k:64 * (k + 1)].astype(BF)
    cw_ref[27] = jnp.zeros((64, 256), BF)
    for t in range(T):
        acc = None
        for dt in range(3):
            if t + 2 - dt >= T:
                continue
            d = dot(w_ref[dt], dc_ref[:, t + 2 - dt].reshape(256, LP))
            acc = d if acc is None else acc + d
        total = None
        for dw in range(3):
            rows = None
            for dr in range(3):
                k = 3 * dr + dw
                s = row_shift(acc[64 * k:64 * (k + 1)], 1 - dr, m)
                rows = s if rows is None else rows + s
            s = col_shift(rows, 1 - dw, m)
            total = s if total is None else total + s
        for h in range(2):
            df_ref[h, t] = total[32 * h:32 * (h + 1)]
            db_ref[h, t] = total[32 * h:32 * (h + 1)].astype(BF)


def backward(dc, pat, w2):
    return pl.pallas_call(
        backward_body,
        out_shape=(
            jax.ShapeDtypeStruct((4 * G, 64, 256), BF),
            jax.ShapeDtypeStruct((2, T, 32, LP), F32),
            jax.ShapeDtypeStruct((2, T, 32, LP), BF),
        ),
        in_specs=[VM] * 3, out_specs=(VM,) * 3,
        compiler_params=params(), name="backward",
    )(dc, pat, w2)


def exchange_out_body(df_ref, db_ref, act_ref, bt_ref, mask_ref, dst, emb_ref, rx, src, ssem, rsem):
    me, z, y, c = shard_spot()
    barrier([("shard", (me + d) % NS) for d in range(1, NS)])
    pair = rcopy(db_ref.at[1 - c], rx, ssem.at[0], rsem.at[0], "shard", sid(z, y, 1 - c))
    pair.start()
    pair.wait_recv()
    emb = jnp.zeros((32, 32), F32)
    for t in range(T):
        g = (df_ref[c, t] + rx[t].astype(F32)).astype(BF).astype(F32) * mask_ref[t]
        emb = emb + dot_nt(bt_ref[t], g.astype(BF))
        both = jnp.concatenate([act_ref[t].astype(F32), g, jnp.zeros((64, LP), F32)], axis=0)
        src[:, 32 * t:32 * (t + 1), :] = jnp.transpose(both).astype(BF).reshape(NS, 32, 128)
    emb_ref[...] = emb
    sends = []
    for d in range(1, NS):
        peer = (me + d) % NS
        cp = rcopy(src.at[peer], dst.at[me], ssem.at[d], rsem.at[d], "shard", peer)
        cp.start()
        sends.append(cp)
    dst[me] = src[me]
    for d in range(1, NS):
        frm = (me + NS - d) % NS
        rcopy(src.at[frm], dst.at[frm], ssem.at[d], rsem.at[d], "shard", frm).wait_recv()
    for cp in sends:
        cp.wait_send()
    pair.wait_send()


def exchange_out(df, db, act, bt, mask):
    return pl.pallas_call(
        exchange_out_body,
        out_shape=(
            jax.ShapeDtypeStruct((NS, 32 * T, 128), BF),
            jax.ShapeDtypeStruct((32, 32), F32),
        ),
        in_specs=[VM] * 5, out_specs=(VM, VM),
        scratch_shapes=[
            pltpu.VMEM((T, 32, LP), BF),
            pltpu.VMEM((NS, 32 * T, 128), BF),
            pltpu.SemaphoreType.DMA((NS,)),
            pltpu.SemaphoreType.DMA((NS,)),
        ],
        compiler_params=params(3), name="exchange_out",
    )(df, db, act, bt, mask)


def reduce_body(cw, sm, fin, smo, out, rx1, tx2, rx2, sx, rz, xb, zb, ssem, rsem, smss, smrs):
    me, z, y, c = shard_spot()
    dp = lax.axis_index("dp")
    x, l = dp // 4, dp % 4
    xp, xm, far = (x + 1) % 4, (x + 3) % 4, (x + 2) % 4
    fwd, bwd = xp * 4 + l, xm * 4 + l
    pair = sid(z, y, 1 - c)
    lines = [x * 4 + (l + k) % 4 for k in range(1, 4)]
    rings = [((x + k) % 4) * 4 + l for k in range(1, 4)]
    barrier(
        [("dp", p) for p in rings] + [("dp", p) for p in lines]
        + [("shard", (me + d) % NS) for d in range(1, NS)]
    )

    def cp(kind, g, src, dst, peer, axis="dp"):
        return rcopy(src, dst, ssem.at[kind, g], rsem.at[kind, g], axis, peer)

    lo4, hi4 = pl.ds(0, 2), pl.ds(2, 2)

    def send(kind, g):
        if kind == 0:
            return cp(0, g, cw.at[g, far, lo4], rx1.at[0, g], fwd)
        if kind == 1:
            return cp(1, g, cw.at[g, far, hi4], rx1.at[1, g], bwd)
        if kind == 2:
            return cp(2, g, tx2.at[0, g], rx2.at[0, g], fwd)
        if kind == 3:
            return cp(3, g, tx2.at[1, g], rx2.at[1, g], bwd)
        if kind in (4, 5, 6):
            k = kind - 3
            return cp(kind, g, sx.at[g, (l + k) % 4], rz.at[g, k], x * 4 + (l + k) % 4)
        if kind in (7, 8, 9):
            k = kind - 6
            return cp(kind, g, out.at[g, x, l], out.at[g, x, l], x * 4 + (l + k) % 4)
        if kind == 10:
            return cp(10, g, out.at[g, x], out.at[g, x], fwd)
        if kind == 11:
            return cp(11, g, out.at[g, x], out.at[g, x], bwd)
        if kind == 12:
            return cp(12, g, out.at[g, xm, lo4], out.at[g, xm, lo4], fwd)
        if kind == 13:
            return cp(13, g, out.at[g, xp, hi4], out.at[g, xp, hi4], bwd)
        return cp(14, g, out.at[g, :, pl.ds(2 * (1 - c), 2)], fin.at[c, g], pair, "shard")

    def got(kind, g):
        if kind in (0, 1):
            ref = rx1.at[kind, g]
        elif kind in (2, 3):
            ref = rx2.at[kind - 2, g]
        elif kind in (4, 5, 6):
            ref = rz.at[g, kind - 3]
        elif kind in (7, 8, 9):
            ref = out.at[g, x, (l + 10 - kind) % 4]
        elif kind == 10:
            ref = out.at[g, xm]
        elif kind == 11:
            ref = out.at[g, xp]
        elif kind == 12:
            ref = out.at[g, far, lo4]
        elif kind == 13:
            ref = out.at[g, far, hi4]
        else:
            ref = fin.at[1 - c, g]
        cp(kind, g, ref, ref, fwd).wait_recv()

    def s1(g):
        send(0, g).start()
        send(1, g).start()

    def s2(g):
        got(0, g)
        tx2[0, g, 0:2] = (cw[g, xp, 0:2].astype(F32) + rx1[0, g].astype(F32)).astype(BF)
        tx2[0, g, 2:4] = cw[g, xp, 2:4]
        send(2, g).start()
        got(1, g)
        tx2[1, g, 2:4] = (cw[g, xm, 2:4].astype(F32) + rx1[1, g].astype(F32)).astype(BF)
        tx2[1, g, 0:2] = cw[g, xm, 0:2]
        send(3, g).start()

    def s3(g):
        got(2, g)
        got(3, g)
        sx[g] = (cw[g, x].astype(F32) + rx2[0, g].astype(F32) + rx2[1, g].astype(F32)).astype(BF)
        for k in (4, 5, 6):
            send(k, g).start()

    def s4(g):
        for k in (4, 5, 6):
            got(k, g)
        tot = sx[g, l].astype(F32) + rz[g, 1].astype(F32) + rz[g, 2].astype(F32) + rz[g, 3].astype(F32)
        out[g, x, l] = tot.astype(BF)
        for k in (7, 8, 9):
            send(k, g).start()

    def s5(g):
        for k in (7, 8, 9):
            got(k, g)
        send(10, g).start()
        send(11, g).start()

    def s6(g):
        got(10, g)
        send(12, g).start()
        got(11, g)
        send(13, g).start()

    def s7(g):
        got(12, g)
        got(13, g)
        send(14, g).start()
        fin[c, g] = out[g, :, pl.ds(2 * c, 2)]

    def small(kind, k, src, dst, axis, peer):
        return rcopy(src, dst, smss.at[kind, k], smrs.at[kind, k], axis, peer)

    def sm1():
        xb[x] = sm[...]
        for k in range(1, 4):
            small(0, k, sm, xb.at[x], "dp", ((x + k) % 4) * 4 + l).start()

    def sm2():
        for k in range(1, 4):
            small(0, k, sm, xb.at[(x + 4 - k) % 4], "dp", fwd).wait_recv()
        zb[l] = (xb[0] + xb[1]) + (xb[2] + xb[3])
        for k in range(1, 4):
            small(1, k, zb.at[l], zb.at[l], "dp", x * 4 + (l + k) % 4).start()

    def sm3():
        for k in range(1, 4):
            small(1, k, zb.at[l], zb.at[(l + 4 - k) % 4], "dp", fwd).wait_recv()
        smo[me] = (zb[0] + zb[1]) + (zb[2] + zb[3])
        for d in range(1, NS):
            small(2, d, smo.at[me], smo.at[me], "shard", (me + d) % NS).start()

    def sm4():
        for d in range(1, NS):
            small(2, d, smo.at[me], smo.at[(me + NS - d) % NS], "shard", (me + 1) % NS).wait_recv()

    stages = (s1, s2, s3, s4, s5, s6, s7)
    sm1()
    for step in range(G + 6):
        if step == 2:
            sm2()
        if step == 5:
            sm3()
        for k in range(7):
            g = step - k
            if 0 <= g < G:
                stages[k](g)
    sm4()
    for g in range(G):
        got(14, g)
        for kind in range(15):
            send(kind, g).wait_send()
    for k in range(1, 4):
        small(0, k, sm, xb.at[x], "dp", fwd).wait_send()
        small(1, k, zb.at[l], zb.at[l], "dp", fwd).wait_send()
    for d in range(1, NS):
        small(2, d, smo.at[me], smo.at[me], "shard", (me + d) % NS).wait_send()


def reduce(cw, sm):
    piece = (16, 256)
    return pl.pallas_call(
        reduce_body,
        out_shape=(
            jax.ShapeDtypeStruct((2, G, 4, 2) + piece, BF),
            jax.ShapeDtypeStruct((NS, 8, 128), F32),
        ),
        in_specs=[VM, VM], out_specs=(VM, VM),
        scratch_shapes=[
            pltpu.VMEM((G, 4, 4) + piece, BF),
            pltpu.VMEM((2, G, 2) + piece, BF),
            pltpu.VMEM((2, G, 4) + piece, BF),
            pltpu.VMEM((2, G, 4) + piece, BF),
            pltpu.VMEM((G, 4) + piece, BF),
            pltpu.VMEM((G, 4) + piece, BF),
            pltpu.VMEM((4, 8, 128), F32),
            pltpu.VMEM((4, 8, 128), F32),
            pltpu.SemaphoreType.DMA((15, G)),
            pltpu.SemaphoreType.DMA((15, G)),
            pltpu.SemaphoreType.DMA((3, NS)),
            pltpu.SemaphoreType.DMA((3, NS)),
        ],
        compiler_params=params(4), name="reduce",
    )(cw, sm)


def on_device(codes, lengths, hidden, embed, conv_weight, gain, bias, cotangent):
    me = lax.axis_index("shard")
    z, y, c = me // 8, (me // 2) % 4, me % 2
    pos = T * R * WD
    frame_mask = (jnp.arange(T) < lengths[0]).astype(F32)
    powers = 2 ** jnp.arange(CODE_BITS, dtype=jnp.int32)
    bits = (codes[0][..., None] // powers % 2 * 2 - 1).astype(BF)
    embedded = jnp.dot(bits.reshape(pos, CODE_BITS), embed, preferred_element_type=F32)
    cell = jnp.repeat(frame_mask, R * WD)[:, None]
    feats = ((embedded + hidden[0].reshape(pos, 512).astype(F32)) * cell).astype(BF)
    by_chip = feats.reshape(pos, 8, 1, 64).transpose(1, 2, 0, 3)
    by_chip = jnp.broadcast_to(by_chip, (8, 2, pos, 64)).reshape(NS, pos, 64)
    ups = (
        cotangent[0].reshape(T, R, 2, WD, 2, 4, 32)
        .transpose(4, 5, 2, 0, 1, 3, 6).reshape(NS, pos, 32)
    )
    bcast = jnp.broadcast_to(bits.reshape(1, pos, CODE_BITS), (NS, pos, CODE_BITS))
    blocks = jnp.concatenate([by_chip, ups, bcast, jnp.zeros((NS, pos, 14), BF)], axis=2)
    g = exchange_in(blocks)
    w = conv_weight.transpose(1, 0, 2)
    mine = lax.dynamic_slice_in_dim(w, 256 * c, 256, 2)
    give = lax.dynamic_slice_in_dim(w, 256 * (1 - c), 256, 2)
    take = lax.ppermute(give, "shard", [(i, i ^ 1) for i in range(NS)])
    first = jnp.where(c == 0, mine, take)
    second = jnp.where(c == 0, take, mine)
    w2 = jnp.concatenate([first, second], axis=1).reshape(3, 576, 256)
    wt = w2.transpose(0, 2, 1)
    part, ut, bt, pat = forward(g, wt)
    conv = scatter(part.reshape(2, 4, T, 32, LP))
    lo = 256 * c + 32 * (4 * z + y)
    own_gain = lax.dynamic_slice_in_dim(gain, lo, 32).reshape(32, 1)
    own_bias = lax.dynamic_slice_in_dim(bias, lo, 32).reshape(32, 1)
    act, dconv, gb = norm(lengths, conv, ut, own_gain, own_bias)
    dc = gather(dconv)
    cw, df, db = backward(dc.reshape(8, T, 32, LP), pat, w2)
    maskv = jnp.broadcast_to(frame_mask[:, None, None], (T, 1, LP))
    back, emb = exchange_out(df, db, act, bt, maskv)
    sm = jnp.concatenate([emb[:CODE_BITS], gb[:, :2].T, jnp.zeros((12, 32), F32)], axis=0)
    sm = sm.reshape(4, 8, 32).transpose(1, 0, 2).reshape(8, 128)
    fin, smo = reduce(cw.reshape(G, 4, 4, 16, 256), sm)
    grad_conv = (
        fin.reshape(2, 4 * G, 32, 256)[:, :27].transpose(2, 1, 0, 3).reshape(32, 27, 512).astype(F32)
    )
    sums = smo.reshape(NS, 8, 4, 32).transpose(2, 1, 0, 3).reshape(32, NS, 32)
    grad_embed = sums[:CODE_BITS].reshape(CODE_BITS, 512)

    def by_owner(v):
        return v.reshape(2, 4, 2, 32).transpose(2, 0, 1, 3).reshape(512)

    back = back.reshape(2, 4, 2, T, R, WD, 128)
    decoded = (
        back[..., 0:32].transpose(3, 4, 2, 5, 0, 1, 6).reshape(1, T, 2 * R, 2 * WD, 128)
    )
    grad_hidden = (
        back[..., 32:64].transpose(3, 4, 5, 0, 1, 2, 6).reshape(1, T, R, WD, 512)
    )
    return (
        decoded, grad_hidden, grad_conv, grad_embed,
        by_owner(sums[CODE_BITS]), by_owner(sums[CODE_BITS + 1]),
    )


def solution(mesh):
    return jax.shard_map(
        on_device,
        mesh=mesh,
        in_specs=(
            P("dp", None, None, "shard"),
            P("dp"),
            P("dp", None, None, "shard", None),
            P(),
            P("shard", None, None),
            P(),
            P(),
            P("dp", None, None, "shard", None),
        ),
        out_specs=(
            P("dp", None, None, "shard", None),
            P("dp", None, None, "shard", None),
            P("shard", None, None),
            P(),
            P(),
            P(),
        ),
        check_vma=False,
    )
```

```python
import jax
import jax.numpy as jnp
from jax import lax
from jax.experimental import pallas as pl
from jax.experimental.pallas import tpu as pltpu
from jax.sharding import PartitionSpec as P

BF = jnp.bfloat16
F32 = jnp.float32
CODE_BITS = 18
EPS = 1e-05
T = 5
R = 8
WD = 4
NS = 16
LP = 512
G = 7
MESH = pl.DeviceIdType.MESH
VM = pl.BlockSpec(memory_space=pltpu.VMEM)


def params(cid=None):
    if cid is None:
        return pltpu.CompilerParams(vmem_limit_bytes=60 * 1024 * 1024)
    return pltpu.CompilerParams(
        vmem_limit_bytes=60 * 1024 * 1024, collective_id=cid, has_side_effects=True
    )


def shard_spot():
    me = lax.axis_index("shard")
    return me, me // 8, (me // 2) % 4, me % 2


def sid(z, y, c):
    return z * 8 + y * 2 + c


def rcopy(src, dst, ssem, rsem, axis, peer):
    return pltpu.make_async_remote_copy(
        src_ref=src, dst_ref=dst, send_sem=ssem, recv_sem=rsem,
        device_id={axis: peer}, device_id_type=MESH,
    )


def lane_masks():
    lane = lax.broadcasted_iota(jnp.int32, (1, LP), 1)
    row = (lane // 4) % 8
    col = lane % 4
    return {
        "r0": row >= 1, "r2": row <= 6,
        "c0": col >= 1, "c2": col <= 2,
        "w0": lane % 4 + lane // 32 > 0, "w2": lane % 4 + 4 * (lane // 32) < 63,
    }


def row_shift(x, d, m):
    if d < 0:
        return jnp.where(m["r0"], pltpu.roll(x, 4, 1), 0.0)
    if d > 0:
        return jnp.where(m["r2"], pltpu.roll(x, LP - 4, 1), 0.0)
    return x


def col_shift(x, d, m):
    if d < 0:
        y = jnp.where(m["c0"], pltpu.roll(x, 1, 1), pltpu.roll(x, 29, 1))
        return jnp.where(m["w0"], y, 0.0)
    if d > 0:
        y = jnp.where(m["c2"], pltpu.roll(x, LP - 1, 1), pltpu.roll(x, LP - 29, 1))
        return jnp.where(m["w2"], y, 0.0)
    return x


def dot(a, b):
    return lax.dot_general(a, b, (((1,), (0,)), ((), ())), preferred_element_type=F32)


def dot_nt(a, b):
    return lax.dot_general(a, b, (((1,), (1,)), ((), ())), preferred_element_type=F32)


class Wires:
    def __init__(self, ss, rs):
        self.ss, self.rs, self.ids, self.started = ss, rs, {}, []

    def make(self, name, src, dst, axis, peer):
        n = self.ids.setdefault(name, len(self.ids))
        return rcopy(src, dst, self.ss.at[n], self.rs.at[n], axis, peer)

    def send(self, name, src, dst, axis, peer):
        cp = self.make(name, src, dst, axis, peer)
        cp.start()
        self.started.append(cp)

    def got(self, name, ref):
        self.make(name, ref, ref, "shard", (lax.axis_index("shard") + 1) % NS).wait_recv()

    def finish(self):
        for cp in self.started:
            cp.wait_send()


N_WIRES = 260


def group_sum(x):
    s = jnp.sum(x, axis=1, keepdims=True)
    g = jnp.sum(s.reshape(2, 16, 1), axis=1, keepdims=True)
    return jnp.broadcast_to(g, (2, 16, 1)).reshape(32, 1)


def picks(rows, period):
    ch = lax.broadcasted_iota(jnp.int32, (rows, 128), 0)
    lane = lax.broadcasted_iota(jnp.int32, (rows, 128), 1)
    return (lane % period == ch).astype(F32).astype(BF)


def block_body(
    fe, up, bp, w, gbv, mk,
    dec, gh, fin, smo,
    fsrc, fbuf, u1, u2s, u2, bits, w2s, wts, pat, part, rx1, tx2, rx2, txz, rxz, conv,
    ut, nrm, dpr, act, own, dcs, wacc, cw, df, db, drx, dft, d1s, d1, d2s, d2,
    out, qx1, qt2, qx2, sx, rz, sm, xb, zb, ss, rs,
):
    me, z, y, c = shard_spot()
    dp = lax.axis_index("dp")
    x, l = dp // 4, dp % 4
    o = 1 - z
    yp, ym, far = (y + 1) % 4, (y + 3) % 4, (y + 2) % 4
    up_id, down_id, over, pair = sid(z, yp, c), sid(z, ym, c), sid(o, y, c), sid(z, y, 1 - c)
    xp, xm, xf = (x + 1) % 4, (x + 3) % 4, (x + 2) % 4
    fwd, bwd = xp * 4 + l, xm * 4 + l
    wires = Wires(ss, rs)
    send, got = wires.send, wires.got
    m = lane_masks()
    lane = lax.broadcasted_iota(jnp.int32, (1, 128), 1)
    grp = [(lane // 32 == g).astype(F32) for g in range(4)]
    grpb = [v.astype(BF) for v in grp]
    half = [(lane // 64 == g).astype(F32) for g in range(2)]
    halfb = [v.astype(BF) for v in half]

    barrier_sem = pltpu.get_barrier_semaphore()
    peers = [("shard", (me + d) % NS) for d in range(1, NS)]
    peers += [("dp", ((x + k) % 4) * 4 + l) for k in range(1, 4)]
    peers += [("dp", x * 4 + (l + k) % 4) for k in range(1, 4)]
    for axis, peer in peers:
        pl.semaphore_signal(barrier_sem, inc=1, device_id={axis: peer}, device_id_type=MESH)

    for col in range(4):
        a = fe[0:80, 128 * col:128 * (col + 1)].astype(F32)
        b = fe[80:160, 128 * col:128 * (col + 1)].astype(F32)
        fsrc[2 * col] = (a * half[0] + pltpu.roll(b, 64, 1) * half[1]).astype(BF)
        fsrc[2 * col + 1] = (pltpu.roll(a, 64, 1) * half[0] + b * half[1]).astype(BF)
    chip = 4 * z + y
    fbuf[me] = fsrc[chip]
    u1[2 * z + c] = up[2 * c + z]
    bits[z, y, c] = bp[...]
    pl.semaphore_wait(barrier_sem, len(peers))

    steps = [(0, 1), (0, 3), (1, 0), (0, 2), (1, 1), (1, 3), (1, 2)]
    for dz, dy in steps:
        zz, yy = (z + dz) % 2, (y + dy) % 4
        send(("f", dz, dy), fsrc.at[4 * zz + yy], fbuf.at[me], "shard", sid(zz, yy, c))
    send("fp", fbuf.at[me], fbuf.at[me], "shard", pair)
    send("w", w.at[:, :, pl.ds(pl.multiple_of(256 * (1 - c), 256), 256)], w2s.at[:, c], "shard", pair)
    trio = [(0, 1), (1, 0), (1, 1)]
    for dz, dc in trio:
        zz, cc = (z + dz) % 2, (c + dc) % 2
        send(("u1", dz, dc), up.at[2 * cc + zz], u1.at[2 * z + c], "shard", sid(zz, y, cc))
        send(("b1", dz, dc), bp, bits.at[z, y, c], "shard", sid(zz, y, cc))
    w2s[:, c] = w[:, :, pl.ds(pl.multiple_of(256 * c, 256), 256)]
    got("w", w2s.at[:, 1 - c])
    for dt in range(3):
        wts[dt] = jnp.transpose(w2s[9 * dt:9 * dt + 9].reshape(576, 256).astype(F32)).astype(BF)
    for dz, dy in steps:
        frm = sid((z + dz) % 2, (y + 4 - dy) % 4, c)
        got(("f", dz, dy), fbuf.at[frm])
        send(("fr", dz, dy), fbuf.at[frm], fbuf.at[frm], "shard", pair)
    got("fp", fbuf.at[pair])
    for dz, dy in steps:
        got(("fr", dz, dy), fbuf.at[sid((z + dz) % 2, (y + 4 - dy) % 4, 1 - c)])

    sel64, sel32 = picks(64, 64), picks(32, 32)

    def features(t):
        pieces = []
        for h in range(2):
            p = 32 * t + 16 * h
            k = p // 80
            p = p - 80 * k
            pieces.append(fbuf[:, p:p + 16, :] * halfb[k][None])
        rows = jnp.concatenate(pieces, axis=1).reshape(LP, 128)
        f = dot_nt(sel64, rows)
        for dw in range(3):
            fc = col_shift(f, dw - 1, m)
            for dr in range(3):
                k = 3 * dr + dw
                pat[t, 64 * k:64 * (k + 1), :] = row_shift(fc, dr - 1, m).astype(BF)

    def comp(t):
        features(t)
        acc = None
        for dt in range(3):
            if t - 2 + dt >= 0:
                d = dot(wts[dt], pat[t - 2 + dt])
                acc = d if acc is None else acc + d
        for k in range(8):
            part[k // 4, k % 4, t] = acc[32 * k:32 * (k + 1)].astype(BF)
        send(("s1a", t), part.at[:, far, t, pl.ds(0, 16)], rx1.at[0, t], "shard", up_id)
        send(("s1b", t), part.at[:, far, t, pl.ds(16, 16)], rx1.at[1, t], "shard", down_id)

    def s2(t):
        got(("s1a", t), rx1.at[0, t])
        tx2[0, t, :, 0:16] = (part[:, yp, t, 0:16].astype(F32) + rx1[0, t].astype(F32)).astype(BF)
        tx2[0, t, :, 16:32] = part[:, yp, t, 16:32]
        send(("s2a", t), tx2.at[0, t], rx2.at[0, t], "shard", up_id)
        got(("s1b", t), rx1.at[1, t])
        tx2[1, t, :, 16:32] = (part[:, ym, t, 16:32].astype(F32) + rx1[1, t].astype(F32)).astype(BF)
        tx2[1, t, :, 0:16] = part[:, ym, t, 0:16]
        send(("s2b", t), tx2.at[1, t], rx2.at[1, t], "shard", down_id)

    def s3(t):
        got(("s2a", t), rx2.at[0, t])
        got(("s2b", t), rx2.at[1, t])
        txz[t] = (
            part[o, y, t].astype(F32) + rx2[0, t, o].astype(F32) + rx2[1, t, o].astype(F32)
        ).astype(BF)
        send(("s3", t), txz.at[t], rxz.at[t], "shard", over)
        conv[t] = part[z, y, t].astype(F32) + rx2[0, t, z].astype(F32) + rx2[1, t, z].astype(F32)

    def s4(t):
        got(("s3", t), rxz.at[t])
        conv[t] = conv[t] + rxz[t].astype(F32)

    def u_second():
        for dz, dc in trio:
            zz, cc = (z + dz) % 2, (c + dc) % 2
            got(("u1", dz, dc), u1.at[2 * zz + cc])
            got(("b1", dz, dc), bits.at[zz, y, cc])
        for q in range(4):
            acc = None
            for g in range(4):
                v = u1[g].astype(F32)
                v = v if g == q else pltpu.roll(v, (32 * (g - q)) % 128, 1)
                acc = v * grp[g] if acc is None else acc + v * grp[g]
            u2s[q] = acc.astype(BF)
        for dy in (1, 3, 2):
            yy = (y + dy) % 4
            send(("u2", dy), u2s.at[yy], u2.at[y], "shard", sid(z, yy, c))
            send(("b2", dy), bits.at[:, y], bits.at[:, y], "shard", sid(z, yy, c))
        u2[y] = u2s[y]

    def u_third():
        for dy in (1, 3, 2):
            got(("u2", dy), u2.at[(y + 4 - dy) % 4])
            got(("b2", dy), bits.at[:, (y + 4 - dy) % 4])
        for t in range(T):
            blocks = []
            for s in range(NS):
                blocks.append(u2[(s // 2) % 4, 32 * t:32 * t + 32, :] * grpb[2 * (s // 8) + s % 2])
            ut[t] = dot_nt(sel32, jnp.concatenate(blocks, axis=0))

    def run(events):
        for _, _, f, args in sorted(events, key=lambda e: e[:2]):
            f(*args)

    ev = []
    for t in range(T):
        ev += [
            (1.5 * t, 0, comp, (t,)), (2.6 + 2.1 * t, 1, s2, (t,)),
            (5.2 + 2.1 * t, 2, s3, (t,)), (11.0 + 2.1 * t, 3, s4, (t,)),
        ]
    ev += [(3.1, 9, u_second, ()), (8.0, 9, u_third, ())]
    run(ev)

    count = (mk[0, :, 0:1] + mk[1, :, 0:1] + mk[2, :, 0:1] + mk[3, :, 0:1] + mk[4, :, 0:1]) * float(R * WD * NS * 16)
    s_one = jnp.zeros((32, LP), F32)
    s_two = jnp.zeros((32, LP), F32)
    for t in range(T):
        v = conv[t] * mk[t]
        s_one = s_one + v
        s_two = s_two + conv[t] * v
    mean = group_sum(s_one) / count
    inv = lax.rsqrt(group_sum(s_two) / count - mean * mean + EPS)
    spot = 8 * c + chip
    gain, bias = gbv[0, spot], gbv[1, spot]
    a1 = jnp.zeros((32, LP), F32)
    a2 = jnp.zeros((32, LP), F32)
    for t in range(T):
        n = (conv[t] - mean) * inv
        pre = n * gain + bias
        sg = jax.nn.sigmoid(pre)
        act[t] = pre * sg * mk[t]
        d = ut[t] * mk[t] * sg * (1.0 + pre * (1.0 - sg))
        a1 = a1 + d
        a2 = a2 + d * n
        nrm[t] = n
        dpr[t] = d
    bterm = jnp.sum(a1, axis=1, keepdims=True)
    gterm = jnp.sum(a2, axis=1, keepdims=True)
    t1 = group_sum(gain * bterm) / count
    t2 = group_sum(gain * gterm) / count

    lo, hi = pl.ds(0, 16), pl.ds(16, 16)
    order = [4, 3, 2, 1, 0]
    for t in order:
        own[t] = (inv * (dpr[t] * gain - t1 - nrm[t] * t2) * mk[t]).astype(BF)
        send(("g0", t), own.at[t], dcs.at[z, y, t], "shard", over)
        send(("g1", t), own.at[t], dcs.at[z, y, t], "shard", up_id)
        send(("g2", t), own.at[t], dcs.at[z, y, t], "shard", down_id)
    for t in order:
        dcs[z, y, t] = own[t]

    def first_out(kind, get):
        for t in range(T):
            v = get(t)
            nat = jnp.transpose(jnp.concatenate([v, v, v, v], axis=0))
            for q in range(4):
                acc = None
                for g in range(4):
                    r0 = 32 * sid(g // 2, q, g % 2)
                    piece = nat[r0:r0 + 32] * grp[g]
                    acc = piece if acc is None else acc + piece
                d1s[kind, q, 32 * t:32 * t + 32, :] = acc.astype(BF)
        for dy in (1, 3, 2):
            yy = (y + dy) % 4
            send(("d1", kind, dy), d1s.at[kind, yy], d1.at[kind, y], "shard", sid(z, yy, c))
        d1[kind, y] = d1s[kind, y]

    def second_out(kind, dst):
        for dy in (1, 3, 2):
            got(("d1", kind, dy), d1.at[kind, (y + 4 - dy) % 4])
        for g in range(4):
            acc = None
            for q in range(4):
                v = d1[kind, q].astype(F32)
                v = v if g == q else pltpu.roll(v, (32 * (q - g)) % 128, 1)
                acc = v * grp[q] if acc is None else acc + v * grp[q]
            d2s[kind, g] = acc.astype(BF)
        for dz, dc in trio:
            zz, cc = (z + dz) % 2, (c + dc) % 2
            send(("d2", kind, dz, dc), d2s.at[kind, 2 * zz + cc], dst.at[2 * z + c], "shard", sid(zz, y, cc))
        dst[2 * z + c] = d2s[kind, 2 * z + c]

    def third_out(kind, dst):
        for dz, dc in trio:
            got(("d2", kind, dz, dc), dst.at[2 * ((z + dz) % 2) + (c + dc) % 2])

    def g_near(t):
        got(("g1", t), dcs.at[z, ym, t])
        send(("g3", t), dcs.at[z, ym, t, lo], dcs.at[z, ym, t, lo], "shard", up_id)
        got(("g2", t), dcs.at[z, yp, t])
        send(("g4", t), dcs.at[z, yp, t, hi], dcs.at[z, yp, t, hi], "shard", down_id)

    def g_over(t):
        got(("g0", t), dcs.at[o, y, t])
        send(("g5", t), dcs.at[o, y, t], dcs.at[o, y, t], "shard", up_id)
        send(("g6", t), dcs.at[o, y, t], dcs.at[o, y, t], "shard", down_id)

    def g_far(t):
        got(("g5", t), dcs.at[o, ym, t])
        send(("g7", t), dcs.at[o, ym, t, lo], dcs.at[o, ym, t, lo], "shard", up_id)
        got(("g6", t), dcs.at[o, yp, t])
        send(("g8", t), dcs.at[o, yp, t, hi], dcs.at[o, yp, t, hi], "shard", down_id)

    def g_done(t):
        got(("g3", t), dcs.at[z, far, t, lo])
        got(("g4", t), dcs.at[z, far, t, hi])
        got(("g7", t), dcs.at[o, far, t, lo])
        got(("g8", t), dcs.at[o, far, t, hi])

    def dgrad(t):
        acc = None
        for dt in range(3):
            if t + 2 - dt < T:
                d = dot(w2s[9 * dt:9 * dt + 9].reshape(576, 256), dcs[:, :, t + 2 - dt].reshape(256, LP))
                acc = d if acc is None else acc + d
        total = None
        for dw in range(3):
            rows = None
            for dr in range(3):
                k = 3 * dr + dw
                s = row_shift(acc[64 * k:64 * (k + 1)], 1 - dr, m)
                rows = s if rows is None else rows + s
            s = col_shift(rows, 1 - dw, m)
            total = s if total is None else total + s
        for h in range(2):
            df[h, t] = total[32 * h:32 * (h + 1)]
            db[h, t] = total[32 * h:32 * (h + 1)].astype(BF)
        send(("pair", t), db.at[1 - c, t], drx.at[t], "shard", pair)

    def wgrad(t):
        dct = dcs[:, :, t].reshape(256, LP)
        for dt in range(3):
            if t - 2 + dt < 0:
                continue
            v = dot_nt(pat[t - 2 + dt], dct)
            if t < T - 1:
                v = v + wacc[dt]
            if t == 2 - dt:
                for k in range(9):
                    tap = 9 * dt + k
                    cw[tap // 4, tap % 4] = v[64 * k:64 * (k + 1)].astype(BF).reshape(4, 16, 256)
            else:
                wacc[dt] = v

    def dsum(t):
        got(("pair", t), drx.at[t])
        dft[t] = (df[c, t] + drx[t].astype(F32)).astype(BF).astype(F32) * mk[t]

    lo4, hi4 = pl.ds(0, 2), pl.ds(2, 2)

    def r1(g):
        send(("r0", g), cw.at[g, xf, lo4], qx1.at[0, g], "dp", fwd)
        send(("r1", g), cw.at[g, xf, hi4], qx1.at[1, g], "dp", bwd)

    def r2(g):
        got(("r0", g), qx1.at[0, g])
        qt2[0, g, 0:2] = (cw[g, xp, 0:2].astype(F32) + qx1[0, g].astype(F32)).astype(BF)
        qt2[0, g, 2:4] = cw[g, xp, 2:4]
        send(("r2", g), qt2.at[0, g], qx2.at[0, g], "dp", fwd)
        got(("r1", g), qx1.at[1, g])
        qt2[1, g, 2:4] = (cw[g, xm, 2:4].astype(F32) + qx1[1, g].astype(F32)).astype(BF)
        qt2[1, g, 0:2] = cw[g, xm, 0:2]
        send(("r3", g), qt2.at[1, g], qx2.at[1, g], "dp", bwd)

    def r3(g):
        got(("r2", g), qx2.at[0, g])
        got(("r3", g), qx2.at[1, g])
        sx[g] = (cw[g, x].astype(F32) + qx2[0, g].astype(F32) + qx2[1, g].astype(F32)).astype(BF)
        for k in (3, 2, 1):
            send(("r4", k, g), sx.at[g, (l + k) % 4], rz.at[g, k], "dp", x * 4 + (l + k) % 4)

    def r4(g):
        tot = sx[g, l].astype(F32)
        for k in (1, 2, 3):
            got(("r4", k, g), rz.at[g, k])
            tot = tot + rz[g, k].astype(F32)
        out[g, x, l] = tot.astype(BF)
        for k in (3, 2, 1):
            send(("r7", k, g), out.at[g, x, l], out.at[g, x, l], "dp", x * 4 + (l + k) % 4)

    def r5(g):
        for k in (1, 2, 3):
            got(("r7", k, g), out.at[g, x, (l + 4 - k) % 4])
        send(("r10", g), out.at[g, x], out.at[g, x], "dp", fwd)
        send(("r11", g), out.at[g, x], out.at[g, x], "dp", bwd)

    def r6(g):
        got(("r10", g), out.at[g, xm])
        send(("r12", g), out.at[g, xm, lo4], out.at[g, xm, lo4], "dp", fwd)
        got(("r11", g), out.at[g, xp])
        send(("r13", g), out.at[g, xp, hi4], out.at[g, xp, hi4], "dp", bwd)

    mine = pl.ds(pl.multiple_of(256 * c, 256), 256)
    other = pl.ds(pl.multiple_of(256 * (1 - c), 256), 256)

    def r7(g):
        got(("r12", g), out.at[g, xf, lo4])
        got(("r13", g), out.at[g, xf, hi4])
        send(("r14", g), out.at[g, :, pl.ds(2 * (1 - c), 2)], fin.at[g, :, :, :, mine], "shard", pair)
        fin[g, :, :, :, mine] = out[g, :, pl.ds(2 * c, 2)]

    def m1():
        acc = jnp.zeros((32, 128), F32)
        for t in range(T):
            r0 = 0 if t < 4 else 32
            rows = bits[:, :, :, r0:r0 + 32, :].reshape(LP, 128)
            v = dot(dft[t].astype(BF), rows)
            acc = acc + (v if t % 4 == 0 else pltpu.roll(v, (128 - 32 * (t % 4)) % 128, 1))
        acc = jnp.where(lane < CODE_BITS, acc, 0.0)
        acc = jnp.where(lane == CODE_BITS, gterm, jnp.where(lane == CODE_BITS + 1, bterm, acc))
        e = jnp.transpose(jnp.concatenate([acc, jnp.zeros((96, 128), F32)], axis=0))
        sm[...] = e[0:8] + pltpu.roll(e[8:16], 32, 1) + pltpu.roll(e[16:24], 64, 1)
        xb[x] = sm[...]
        for k in (2, 1, 3):
            send(("m1", k), sm, xb.at[x], "dp", ((x + k) % 4) * 4 + l)

    def m2():
        for k in (1, 2, 3):
            got(("m1", k), xb.at[(x + 4 - k) % 4])
        zb[l] = (xb[0] + xb[1]) + (xb[2] + xb[3])
        for k in (3, 2, 1):
            send(("m2", k), zb.at[l], zb.at[l], "dp", x * 4 + (l + k) % 4)

    def m3():
        for k in (1, 2, 3):
            got(("m2", k), zb.at[(l + 4 - k) % 4])
        smo[me] = (zb[0] + zb[1]) + (zb[2] + zb[3])
        for d in range(1, NS):
            send(("m3", d), smo.at[me], smo.at[me], "shard", (me + d) % NS)

    def m4():
        for d in range(1, NS):
            got(("m3", d), smo.at[(me + NS - d) % NS])

    def last_hidden():
        third_out(1, d2)
        for zz in range(2):
            for h in range(2):
                acc = None
                for g in range(4):
                    v = d2[2 * zz + g % 2].astype(F32)
                    q = 2 * h + g // 2
                    v = v if g == q else pltpu.roll(v, (32 * (g - q)) % 128, 1)
                    acc = v * grp[g] if acc is None else acc + v * grp[g]
                gh[:, 128 * (2 * zz + h):128 * (2 * zz + h + 1)] = acc.astype(BF)

    ev = [(0.1, 0, first_out, (0, lambda t: act[t])), (8.2, 0, second_out, (0, dec))]
    for i, t in enumerate(order):
        ev += [
            (2.4 + 1.1 * i, 1, g_near, (t,)), (5.5 + 1.6 * i, 2, g_over, (t,)),
            (8.5 + 1.6 * i, 3, g_far, (t,)), (11.0 + 2.1 * i, 4, g_done, (t,)),
            (11.0 + 2.1 * i, 5, dgrad, (t,)), (11.0 + 2.1 * i, 6, wgrad, (t,)),
            (13.0 + 2.1 * i, 7, dsum, (t,)),
        ]
    ready = (15.3, 15.4, 17.4, 17.5, 19.5, 19.6, 19.7)
    for g in range(G):
        at = ready[g]
        lag = max(0.0, 15.3 + 1.3 * g - at)
        for off, n, f in ((0.0, 20, r1), (2.2, 21, r2), (4.6, 22, r3), (9.0, 23, r4), (13.5, 24, r5), (16.5, 25, r6), (19.0, 26, r7)):
            ev.append((at + off + (lag if off else 0.0), n, f, (g,)))
    ev += [
        (21.6, 40, m1, ()), (21.7, 41, first_out, (1, lambda t: dft[t])), (25.5, 41, m2, ()), (25.6, 42, second_out, (1, d2)),
        (30.5, 43, m3, ()), (33.0, 44, last_hidden, ()), (37.0, 45, m4, ()), (37.1, 46, third_out, (0, dec)),
    ]
    cw[6, 3] = jnp.zeros((4, 16, 256), BF)
    run(ev)
    for g in range(G):
        got(("r14", g), fin.at[g, :, :, :, other])
    wires.finish()


def block(fe, up, bp, w, gbv, mk):
    v = pltpu.VMEM
    piece = (16, 256)
    return pl.pallas_call(
        block_body,
        out_shape=(
            jax.ShapeDtypeStruct((4, 160, 128), BF),
            jax.ShapeDtypeStruct((160, 512), BF),
            jax.ShapeDtypeStruct((G, 4, 2, 16, 512), BF),
            jax.ShapeDtypeStruct((NS, 8, 128), F32),
        ),
        in_specs=[VM] * 6, out_specs=(VM,) * 4,
        scratch_shapes=[
            v((8, 80, 128), BF), v((NS, 80, 128), BF),
            v((4, 160, 128), BF), v((4, 160, 128), BF), v((4, 160, 128), BF),
            v((2, 4, 2, 64, 128), BF), v((27, 2, 32, 256), BF), v((3, 256, 576), BF),
            v((T, 576, LP), BF), v((2, 4, T, 32, LP), BF),
            v((2, T, 2, 16, LP), BF), v((2, T, 2, 32, LP), BF), v((2, T, 2, 32, LP), BF),
            v((T, 32, LP), BF), v((T, 32, LP), BF), v((T, 32, LP), F32),
            v((T, 32, LP), F32), v((T, 32, LP), F32), v((T, 32, LP), F32), v((T, 32, LP), F32),
            v((T, 32, LP), BF), v((2, 4, T, 32, LP), BF), v((3, 576, 256), F32),
            v((G, 4, 4) + piece, BF),
            v((2, T, 32, LP), F32), v((2, T, 32, LP), BF), v((T, 32, LP), BF), v((T, 32, LP), F32),
            v((2, 4, 160, 128), BF), v((2, 4, 160, 128), BF), v((2, 4, 160, 128), BF), v((4, 160, 128), BF),
            v((G, 4, 4) + piece, BF), v((2, G, 2) + piece, BF), v((2, G, 4) + piece, BF),
            v((2, G, 4) + piece, BF), v((G, 4) + piece, BF), v((G, 4) + piece, BF),
            v((8, 128), F32), v((4, 8, 128), F32), v((4, 8, 128), F32),
            pltpu.SemaphoreType.DMA((N_WIRES,)), pltpu.SemaphoreType.DMA((N_WIRES,)),
        ],
        compiler_params=params(0), name="block",
    )(fe, up, bp, w, gbv, mk)


def on_device(codes, lengths, hidden, embed, conv_weight, gain, bias, cotangent):
    pos = T * R * WD
    frame_mask = (jnp.arange(T) < lengths[0]).astype(F32)
    powers = 2 ** jnp.arange(CODE_BITS, dtype=jnp.int32)
    bits = (codes[0][..., None] // powers % 2 * 2 - 1).astype(BF).reshape(pos, CODE_BITS)
    embedded = jnp.dot(bits, embed, preferred_element_type=F32)
    cell = jnp.repeat(frame_mask, R * WD)[:, None]
    fe = ((embedded + hidden[0].reshape(pos, 512).astype(F32)) * cell).astype(BF)
    up = (
        cotangent[0].reshape(T, R, 2, WD, 2, 128).transpose(2, 4, 0, 1, 3, 5).reshape(4, pos, 128)
    )
    wide = jnp.pad(bits, ((0, 96), (0, 32 - CODE_BITS))).reshape(2, 4, 32, 32)
    bp = wide.transpose(0, 2, 1, 3).reshape(64, 128)
    gbv = jnp.stack([gain, bias]).reshape(2, NS, 32, 1)
    maskv = jnp.broadcast_to(frame_mask[:, None, None], (T, 1, LP))
    dec, gh, fin, smo = block(fe, up, bp, conv_weight.transpose(1, 0, 2), gbv, maskv)
    grad_conv = fin.reshape(4 * G, 32, 512)[:27].astype(F32).transpose(1, 0, 2)
    sums = smo.reshape(NS, 8, 4, 32).transpose(2, 1, 0, 3).reshape(32, NS, 32)
    grad_embed = sums[:CODE_BITS].reshape(CODE_BITS, 512)

    def by_owner(v):
        return v.reshape(2, 4, 2, 32).transpose(2, 0, 1, 3).reshape(512)

    decoded = (
        dec.reshape(2, 2, T, R, WD, 128).transpose(2, 3, 1, 4, 0, 5).reshape(1, T, 2 * R, 2 * WD, 128)
    )
    grad_hidden = gh.reshape(1, T, R, WD, 512)
    return (
        decoded, grad_hidden, grad_conv, grad_embed,
        by_owner(sums[CODE_BITS]), by_owner(sums[CODE_BITS + 1]),
    )


def solution(mesh):
    return jax.shard_map(
        on_device,
        mesh=mesh,
        in_specs=(
            P("dp", None, None, "shard"),
            P("dp"),
            P("dp", None, None, "shard", None),
            P(),
            P("shard", None, None),
            P(),
            P(),
            P("dp", None, None, "shard", None),
        ),
        out_specs=(
            P("dp", None, None, "shard", None),
            P("dp", None, None, "shard", None),
            P("shard", None, None),
            P(),
            P(),
            P(),
        ),
        check_vma=False,
    )
```

```python
import jax
import jax.numpy as jnp
from jax import lax
from jax.experimental import pallas as pl
from jax.experimental.pallas import tpu as pltpu
from jax.sharding import PartitionSpec as P

BF = jnp.bfloat16
F32 = jnp.float32
CODE_BITS = 18
EPS = 1e-05
T = 5
R = 8
WD = 4
NS = 16
LP = 512
G = 7
MESH = pl.DeviceIdType.MESH
VM = pl.BlockSpec(memory_space=pltpu.VMEM)


def params(cid=None):
    if cid is None:
        return pltpu.CompilerParams(vmem_limit_bytes=60 * 1024 * 1024)
    return pltpu.CompilerParams(
        vmem_limit_bytes=60 * 1024 * 1024, collective_id=cid, has_side_effects=True
    )


def shard_spot():
    me = lax.axis_index("shard")
    return me, me // 8, (me // 2) % 4, me % 2


def sid(z, y, c):
    return z * 8 + y * 2 + c


def rcopy(src, dst, ssem, rsem, axis, peer):
    return pltpu.make_async_remote_copy(
        src_ref=src, dst_ref=dst, send_sem=ssem, recv_sem=rsem,
        device_id={axis: peer}, device_id_type=MESH,
    )


def lane_masks():
    lane = lax.broadcasted_iota(jnp.int32, (1, LP), 1)
    row = (lane // 4) % 8
    col = lane % 4
    return {
        "r0": row >= 1, "r2": row <= 6,
        "c0": col >= 1, "c2": col <= 2,
        "w0": lane % 4 + lane // 32 > 0, "w2": lane % 4 + 4 * (lane // 32) < 63,
    }


def row_shift(x, d, m):
    if d < 0:
        return jnp.where(m["r0"], pltpu.roll(x, 4, 1), 0.0)
    if d > 0:
        return jnp.where(m["r2"], pltpu.roll(x, LP - 4, 1), 0.0)
    return x


def col_shift(x, d, m):
    if d < 0:
        y = jnp.where(m["c0"], pltpu.roll(x, 1, 1), pltpu.roll(x, 29, 1))
        return jnp.where(m["w0"], y, 0.0)
    if d > 0:
        y = jnp.where(m["c2"], pltpu.roll(x, LP - 1, 1), pltpu.roll(x, LP - 29, 1))
        return jnp.where(m["w2"], y, 0.0)
    return x


def dot(a, b):
    return lax.dot_general(a, b, (((1,), (0,)), ((), ())), preferred_element_type=F32)


def dot_nt(a, b):
    return lax.dot_general(a, b, (((1,), (1,)), ((), ())), preferred_element_type=F32)


class Wires:
    def __init__(self, ss, rs):
        self.ss, self.rs, self.ids, self.started = ss, rs, {}, []

    def make(self, name, src, dst, axis, peer):
        n = self.ids.setdefault(name, len(self.ids))
        return rcopy(src, dst, self.ss.at[n], self.rs.at[n], axis, peer)

    def send(self, name, src, dst, axis, peer):
        cp = self.make(name, src, dst, axis, peer)
        cp.start()
        self.started.append(cp)

    def got(self, name, ref):
        self.make(name, ref, ref, "shard", (lax.axis_index("shard") + 1) % NS).wait_recv()

    def finish(self):
        for cp in self.started:
            cp.wait_send()


N_WIRES = 260


def group_sum(x):
    s = jnp.sum(x, axis=1, keepdims=True)
    g = jnp.sum(s.reshape(2, 16, 1), axis=1, keepdims=True)
    return jnp.broadcast_to(g, (2, 16, 1)).reshape(32, 1)


def picks(rows, period):
    ch = lax.broadcasted_iota(jnp.int32, (rows, 128), 0)
    lane = lax.broadcasted_iota(jnp.int32, (rows, 128), 1)
    return (lane % period == ch).astype(F32).astype(BF)


def placing(way):
    dst = lax.broadcasted_iota(jnp.int32, (128, 128), way)
    src = lax.broadcasted_iota(jnp.int32, (128, 128), 1 - way)
    a, b, r, w = dst // 64, (dst // 32) % 2, (dst // 4) % 8, dst % 4
    return (src == 16 * r + 8 * a + 2 * w + b).astype(F32).astype(BF)


def block_body(
    length_ref, ci, hid, emb_ref, w, gain_ref, bias_ref, cot,
    dec, gho, fin, smo,
    epad, fe, up, gcol, cbuf, fsrc, fbuf, u1, u2s, u2, w2s, wts, pat, part, rx1, tx2, rx2, txz, rxz, conv,
    ut, nrm, dpr, act, own, dcs, wacc, cw, df, db, drx, dft, d1s, d1, d2s,
    out, qx1, qt2, qx2, sx, rz, sm, xb, zb, ss, rs,
):
    me, z, y, c = shard_spot()
    dp = lax.axis_index("dp")
    x, l = dp // 4, dp % 4
    o = 1 - z
    yp, ym, far = (y + 1) % 4, (y + 3) % 4, (y + 2) % 4
    up_id, down_id, over, pair = sid(z, yp, c), sid(z, ym, c), sid(o, y, c), sid(z, y, 1 - c)
    xp, xm, xf = (x + 1) % 4, (x + 3) % 4, (x + 2) % 4
    fwd, bwd = xp * 4 + l, xm * 4 + l
    wires = Wires(ss, rs)
    send, got = wires.send, wires.got
    m = lane_masks()
    lane = lax.broadcasted_iota(jnp.int32, (1, 128), 1)
    grp = [(lane // 32 == g).astype(F32) for g in range(4)]
    grpb = [v.astype(BF) for v in grp]
    half = [(lane // 64 == g).astype(F32) for g in range(2)]
    halfb = [v.astype(BF) for v in half]

    barrier_sem = pltpu.get_barrier_semaphore()
    peers = [("shard", (me + d) % NS) for d in range(1, NS)]
    peers += [("dp", ((x + k) % 4) * 4 + l) for k in range(1, 4)]
    peers += [("dp", x * 4 + (l + k) % 4) for k in range(1, 4)]
    for axis, peer in peers:
        pl.semaphore_signal(barrier_sem, inc=1, device_id={axis: peer}, device_id_type=MESH)

    length = length_ref[0]
    mk = [jnp.where(t < length, 1.0, 0.0) for t in range(T)]
    bit = lax.broadcasted_iota(jnp.int32, (128, 128), 0)
    epad[...] = jnp.zeros((128, 512), BF)
    epad[0:CODE_BITS] = emb_ref[...]
    for h in range(2):
        code = jnp.broadcast_to(ci[h:h + 1, :], (128, 128))
        signs = jnp.where(bit < CODE_BITS, (lax.shift_right_logical(code, jnp.minimum(bit, 31)) & 1) * 2 - 1, 0)
        nat = dot(jnp.transpose(signs.astype(F32)).astype(BF), epad[...])
        for t in range(4 * h, min(T, 4 * h + 4)):
            r0 = 32 * (t - 4 * h)
            fe[32 * t:32 * t + 32] = (
                (nat[r0:r0 + 32] + hid[32 * t:32 * t + 32].astype(F32)) * mk[t]
            ).astype(BF)
    place = placing(0)
    for t in range(T):
        v = dot(place, cot[128 * t:128 * t + 128]).astype(BF)
        for q in range(4):
            up[q, 32 * t:32 * t + 32] = v[32 * q:32 * q + 32]
    for k, ref in enumerate((gain_ref, bias_ref)):
        gcol[k] = jnp.transpose(jnp.broadcast_to(ref[pl.ds(2 * c + z, 1), :], (128, 128)))

    for col in range(4):
        a = fe[0:80, 128 * col:128 * (col + 1)].astype(F32)
        b = fe[80:160, 128 * col:128 * (col + 1)].astype(F32)
        fsrc[2 * col] = (a * half[0] + pltpu.roll(b, 64, 1) * half[1]).astype(BF)
        fsrc[2 * col + 1] = (pltpu.roll(a, 64, 1) * half[0] + b * half[1]).astype(BF)
    chip = 4 * z + y
    fbuf[me] = fsrc[chip]
    u1[2 * z + c] = up[2 * c + z]
    cbuf[me] = ci[...]
    pl.semaphore_wait(barrier_sem, len(peers))

    steps = [(0, 1), (0, 3), (1, 0), (0, 2), (1, 1), (1, 3), (1, 2)]
    for dz, dy in steps:
        zz, yy = (z + dz) % 2, (y + dy) % 4
        send(("f", dz, dy), fsrc.at[4 * zz + yy], fbuf.at[me], "shard", sid(zz, yy, c))
    send("fp", fbuf.at[me], fbuf.at[me], "shard", pair)
    send("w", w.at[:, :, pl.ds(pl.multiple_of(256 * (1 - c), 256), 256)], w2s.at[:, c], "shard", pair)
    w2s[:, c] = w[:, :, pl.ds(pl.multiple_of(256 * c, 256), 256)]
    got("w", w2s.at[:, 1 - c])
    for dt in range(3):
        wts[dt] = jnp.transpose(w2s[9 * dt:9 * dt + 9].reshape(576, 256).astype(F32)).astype(BF)
    for dz, dy in steps:
        frm = sid((z + dz) % 2, (y + 4 - dy) % 4, c)
        got(("f", dz, dy), fbuf.at[frm])
        send(("fr", dz, dy), fbuf.at[frm], fbuf.at[frm], "shard", pair)
    got("fp", fbuf.at[pair])
    trio = [(0, 1), (1, 0), (1, 1)]
    for dz, dc in trio:
        zz, cc = (z + dz) % 2, (c + dc) % 2
        send(("u1", dz, dc), up.at[2 * cc + zz], u1.at[2 * z + c], "shard", sid(zz, y, cc))
    for d in range(1, NS):
        send(("b", d), ci, cbuf.at[me], "shard", (me + d) % NS)
    for dz, dy in steps:
        got(("fr", dz, dy), fbuf.at[sid((z + dz) % 2, (y + 4 - dy) % 4, 1 - c)])

    sel64, sel32 = picks(64, 64), picks(32, 32)

    def features(t):
        pieces = []
        for h in range(2):
            p = 32 * t + 16 * h
            k = p // 80
            p = p - 80 * k
            pieces.append(fbuf[:, p:p + 16, :] * halfb[k][None])
        rows = jnp.concatenate(pieces, axis=1).reshape(LP, 128)
        f = dot_nt(sel64, rows)
        for dw in range(3):
            fc = col_shift(f, dw - 1, m)
            for dr in range(3):
                k = 3 * dr + dw
                pat[t, 64 * k:64 * (k + 1), :] = row_shift(fc, dr - 1, m).astype(BF)

    def comp(t):
        features(t)
        acc = None
        for dt in range(3):
            if t - 2 + dt >= 0:
                d = dot(wts[dt], pat[t - 2 + dt])
                acc = d if acc is None else acc + d
        for k in range(8):
            part[k // 4, k % 4, t] = acc[32 * k:32 * (k + 1)].astype(BF)
        send(("s1a", t), part.at[:, far, t, pl.ds(0, 16)], rx1.at[0, t], "shard", up_id)
        send(("s1b", t), part.at[:, far, t, pl.ds(16, 16)], rx1.at[1, t], "shard", down_id)

    def s2(t):
        got(("s1a", t), rx1.at[0, t])
        tx2[0, t, :, 0:16] = (part[:, yp, t, 0:16].astype(F32) + rx1[0, t].astype(F32)).astype(BF)
        tx2[0, t, :, 16:32] = part[:, yp, t, 16:32]
        send(("s2a", t), tx2.at[0, t], rx2.at[0, t], "shard", up_id)
        got(("s1b", t), rx1.at[1, t])
        tx2[1, t, :, 16:32] = (part[:, ym, t, 16:32].astype(F32) + rx1[1, t].astype(F32)).astype(BF)
        tx2[1, t, :, 0:16] = part[:, ym, t, 0:16]
        send(("s2b", t), tx2.at[1, t], rx2.at[1, t], "shard", down_id)

    def s3(t):
        got(("s2a", t), rx2.at[0, t])
        got(("s2b", t), rx2.at[1, t])
        txz[t] = (
            part[o, y, t].astype(F32) + rx2[0, t, o].astype(F32) + rx2[1, t, o].astype(F32)
        ).astype(BF)
        send(("s3", t), txz.at[t], rxz.at[t], "shard", over)
        conv[t] = part[z, y, t].astype(F32) + rx2[0, t, z].astype(F32) + rx2[1, t, z].astype(F32)

    def s4(t):
        got(("s3", t), rxz.at[t])
        conv[t] = conv[t] + rxz[t].astype(F32)

    def u_second():
        for dz, dc in trio:
            zz, cc = (z + dz) % 2, (c + dc) % 2
            got(("u1", dz, dc), u1.at[2 * zz + cc])
        for q in range(4):
            acc = None
            for g in range(4):
                v = u1[g].astype(F32)
                v = v if g == q else pltpu.roll(v, (32 * (g - q)) % 128, 1)
                acc = v * grp[g] if acc is None else acc + v * grp[g]
            u2s[q] = acc.astype(BF)
        for dy in (1, 3, 2):
            yy = (y + dy) % 4
            send(("u2", dy), u2s.at[yy], u2.at[y], "shard", sid(z, yy, c))
        u2[y] = u2s[y]

    def u_third():
        for dy in (1, 3, 2):
            got(("u2", dy), u2.at[(y + 4 - dy) % 4])
        for t in range(T):
            blocks = []
            for s in range(NS):
                blocks.append(u2[(s // 2) % 4, 32 * t:32 * t + 32, :] * grpb[2 * (s // 8) + s % 2])
            ut[t] = dot_nt(sel32, jnp.concatenate(blocks, axis=0))

    def run(events):
        for _, _, f, args in sorted(events, key=lambda e: e[:2]):
            f(*args)

    ev = []
    for t in range(T):
        ev += [
            (1.5 * t, 0, comp, (t,)), (2.6 + 2.1 * t, 1, s2, (t,)),
            (5.2 + 2.1 * t, 2, s3, (t,)), (11.0 + 2.1 * t, 3, s4, (t,)),
        ]
    ev += [(7.0, 9, u_second, ()), (14.5, 9, u_third, ())]
    run(ev)

    count = length.astype(F32) * float(R * WD * NS * 16)
    s_one = jnp.zeros((32, LP), F32)
    s_two = jnp.zeros((32, LP), F32)
    for t in range(T):
        v = conv[t] * mk[t]
        s_one = s_one + v
        s_two = s_two + conv[t] * v
    mean = group_sum(s_one) / count
    inv = lax.rsqrt(group_sum(s_two) / count - mean * mean + EPS)
    mine32 = pl.ds(pl.multiple_of(32 * y, 32), 32)
    gain, bias = gcol[0, mine32, 0:1], gcol[1, mine32, 0:1]
    a1 = jnp.zeros((32, LP), F32)
    a2 = jnp.zeros((32, LP), F32)
    for t in range(T):
        n = (conv[t] - mean) * inv
        pre = n * gain + bias
        sg = jax.nn.sigmoid(pre)
        act[t] = pre * sg * mk[t]
        d = ut[t] * mk[t] * sg * (1.0 + pre * (1.0 - sg))
        a1 = a1 + d
        a2 = a2 + d * n
        nrm[t] = n
        dpr[t] = d
    bterm = jnp.sum(a1, axis=1, keepdims=True)
    gterm = jnp.sum(a2, axis=1, keepdims=True)
    t1 = group_sum(gain * bterm) / count
    t2 = group_sum(gain * gterm) / count

    lo, hi = pl.ds(0, 16), pl.ds(16, 16)
    order = [4, 3, 2, 1, 0]
    for t in order:
        own[t] = (inv * (dpr[t] * gain - t1 - nrm[t] * t2) * mk[t]).astype(BF)
        send(("g0", t), own.at[t], dcs.at[z, y, t], "shard", over)
        send(("g1", t), own.at[t], dcs.at[z, y, t], "shard", up_id)
        send(("g2", t), own.at[t], dcs.at[z, y, t], "shard", down_id)
    for t in order:
        dcs[z, y, t] = own[t]

    def first_out(kind, get, t0, t1):
        for t in range(t0, t1):
            v = get(t)
            nat = jnp.transpose(jnp.concatenate([v, v, v, v], axis=0))
            for q in range(4):
                acc = None
                for g in range(4):
                    r0 = 32 * sid(g // 2, q, g % 2)
                    piece = nat[r0:r0 + 32] * grp[g]
                    acc = piece if acc is None else acc + piece
                d1s[kind, q, 32 * t:32 * t + 32, :] = acc.astype(BF)
        for dy in (1, 3, 2):
            yy = (y + dy) % 4
            part_of = pl.ds(32 * t0, 32 * (t1 - t0))
            send(
                ("d1", kind, t0, dy), d1s.at[kind, yy, part_of], d1.at[kind, y, part_of], "shard", sid(z, yy, c)
            )
        d1[kind, y, 32 * t0:32 * t1] = d1s[kind, y, 32 * t0:32 * t1]

    def second_out(kind, dst, t0, t1):
        part_of = pl.ds(32 * t0, 32 * (t1 - t0))
        for dy in (1, 3, 2):
            got(("d1", kind, t0, dy), d1.at[kind, (y + 4 - dy) % 4, part_of])
        for g in range(4):
            acc = None
            for q in range(4):
                v = d1[kind, q, 32 * t0:32 * t1].astype(F32)
                v = v if g == q else pltpu.roll(v, (32 * (q - g)) % 128, 1)
                acc = v * grp[q] if acc is None else acc + v * grp[q]
            d2s[kind, g, 32 * t0:32 * t1] = acc.astype(BF)
        for dz, dc in trio:
            zz, cc = (z + dz) % 2, (c + dc) % 2
            send(
                ("d2", kind, t0, dz, dc), d2s.at[kind, 2 * zz + cc, part_of], dst.at[2 * z + c, part_of],
                "shard", sid(zz, y, cc),
            )
        dst[2 * z + c, 32 * t0:32 * t1] = d2s[kind, 2 * z + c, 32 * t0:32 * t1]

    def third_out(kind, dst, t0, t1):
        part_of = pl.ds(32 * t0, 32 * (t1 - t0))
        for dz, dc in trio:
            got(("d2", kind, t0, dz, dc), dst.at[2 * ((z + dz) % 2) + (c + dc) % 2, part_of])

    def g_near(t):
        got(("g1", t), dcs.at[z, ym, t])
        send(("g3", t), dcs.at[z, ym, t, lo], dcs.at[z, ym, t, lo], "shard", up_id)
        got(("g2", t), dcs.at[z, yp, t])
        send(("g4", t), dcs.at[z, yp, t, hi], dcs.at[z, yp, t, hi], "shard", down_id)

    def g_over(t):
        got(("g0", t), dcs.at[o, y, t])
        send(("g5", t), dcs.at[o, y, t], dcs.at[o, y, t], "shard", up_id)
        send(("g6", t), dcs.at[o, y, t], dcs.at[o, y, t], "shard", down_id)

    def g_far(t):
        got(("g5", t), dcs.at[o, ym, t])
        send(("g7", t), dcs.at[o, ym, t, lo], dcs.at[o, ym, t, lo], "shard", up_id)
        got(("g6", t), dcs.at[o, yp, t])
        send(("g8", t), dcs.at[o, yp, t, hi], dcs.at[o, yp, t, hi], "shard", down_id)

    def g_done(t):
        got(("g3", t), dcs.at[z, far, t, lo])
        got(("g4", t), dcs.at[z, far, t, hi])
        got(("g7", t), dcs.at[o, far, t, lo])
        got(("g8", t), dcs.at[o, far, t, hi])

    def dgrad(t):
        acc = None
        for dt in range(3):
            if t + 2 - dt < T:
                d = dot(w2s[9 * dt:9 * dt + 9].reshape(576, 256), dcs[:, :, t + 2 - dt].reshape(256, LP))
                acc = d if acc is None else acc + d
        total = None
        for dw in range(3):
            rows = None
            for dr in range(3):
                k = 3 * dr + dw
                s = row_shift(acc[64 * k:64 * (k + 1)], 1 - dr, m)
                rows = s if rows is None else rows + s
            s = col_shift(rows, 1 - dw, m)
            total = s if total is None else total + s
        for h in range(2):
            df[h, t] = total[32 * h:32 * (h + 1)]
            db[h, t] = total[32 * h:32 * (h + 1)].astype(BF)
        send(("pair", t), db.at[1 - c, t], drx.at[t], "shard", pair)

    def wgrad(t):
        dct = dcs[:, :, t].reshape(256, LP)
        for dt in range(3):
            if t - 2 + dt < 0:
                continue
            v = dot_nt(pat[t - 2 + dt], dct)
            if t < T - 1:
                v = v + wacc[dt]
            if t == 2 - dt:
                for k in range(9):
                    tap = 9 * dt + k
                    cw[tap // 4, tap % 4] = v[64 * k:64 * (k + 1)].astype(BF).reshape(4, 16, 256)
            else:
                wacc[dt] = v

    def dsum(t):
        got(("pair", t), drx.at[t])
        dft[t] = (df[c, t] + drx[t].astype(F32)).astype(BF).astype(F32) * mk[t]

    lo4, hi4 = pl.ds(0, 2), pl.ds(2, 2)

    def r1(g):
        send(("r0", g), cw.at[g, xf, lo4], qx1.at[0, g], "dp", fwd)
        send(("r1", g), cw.at[g, xf, hi4], qx1.at[1, g], "dp", bwd)

    def r2(g):
        got(("r0", g), qx1.at[0, g])
        qt2[0, g, 0:2] = (cw[g, xp, 0:2].astype(F32) + qx1[0, g].astype(F32)).astype(BF)
        qt2[0, g, 2:4] = cw[g, xp, 2:4]
        send(("r2", g), qt2.at[0, g], qx2.at[0, g], "dp", fwd)
        got(("r1", g), qx1.at[1, g])
        qt2[1, g, 2:4] = (cw[g, xm, 2:4].astype(F32) + qx1[1, g].astype(F32)).astype(BF)
        qt2[1, g, 0:2] = cw[g, xm, 0:2]
        send(("r3", g), qt2.at[1, g], qx2.at[1, g], "dp", bwd)

    def r3(g):
        got(("r2", g), qx2.at[0, g])
        got(("r3", g), qx2.at[1, g])
        sx[g] = (cw[g, x].astype(F32) + qx2[0, g].astype(F32) + qx2[1, g].astype(F32)).astype(BF)
        for k in (3, 2, 1):
            send(("r4", k, g), sx.at[g, (l + k) % 4], rz.at[g, k], "dp", x * 4 + (l + k) % 4)

    def r4(g):
        tot = sx[g, l].astype(F32)
        for k in (1, 2, 3):
            got(("r4", k, g), rz.at[g, k])
            tot = tot + rz[g, k].astype(F32)
        out[g, x, l] = tot.astype(BF)
        for k in (3, 2, 1):
            send(("r7", k, g), out.at[g, x, l], out.at[g, x, l], "dp", x * 4 + (l + k) % 4)

    def r5(g):
        for k in (1, 2, 3):
            got(("r7", k, g), out.at[g, x, (l + 4 - k) % 4])
        send(("r10", g), out.at[g, x], out.at[g, x], "dp", fwd)
        send(("r11", g), out.at[g, x], out.at[g, x], "dp", bwd)

    def r6(g):
        got(("r10", g), out.at[g, xm])
        send(("r12", g), out.at[g, xm, lo4], out.at[g, xm, lo4], "dp", fwd)
        got(("r11", g), out.at[g, xp])
        send(("r13", g), out.at[g, xp, hi4], out.at[g, xp, hi4], "dp", bwd)

    mine = pl.ds(pl.multiple_of(256 * c, 256), 256)
    other = pl.ds(pl.multiple_of(256 * (1 - c), 256), 256)

    def r7(g):
        got(("r12", g), out.at[g, xf, lo4])
        got(("r13", g), out.at[g, xf, hi4])
        send(("r14", g), out.at[g, :, pl.ds(2 * (1 - c), 2)], fin.at[g, :, :, :, mine], "shard", pair)
        fin[g, :, :, :, mine] = out[g, :, pl.ds(2 * c, 2)]

    def m1():
        for d in range(1, NS):
            got(("b", d), cbuf.at[(me + NS - d) % NS])
        grpi = [(lane // 32 == g).astype(jnp.int32) for g in range(4)]
        bit32 = lax.broadcasted_iota(jnp.int32, (32, LP), 0)
        acc = jnp.zeros((32, 128), F32)
        for f in range(4):
            cols = []
            for q in range(4):
                v = None
                for j in range(4):
                    r = cbuf[4 * q + j]
                    r = r if j == f else pltpu.roll(r, (32 * (j - f)) % 128, 1)
                    v = r * grpi[j] if v is None else v + r * grpi[j]
                cols.append(v)
            for t in ((0, 4) if f == 0 else (f,)):
                code = jnp.concatenate([v[t // 4:t // 4 + 1] for v in cols], axis=1)
                code = jnp.broadcast_to(code, (32, LP))
                signs = jnp.where(bit32 < CODE_BITS, (lax.shift_right_logical(code, bit32) & 1) * 2 - 1, 0)
                rhs = jnp.concatenate([dft[t], jnp.zeros((96, LP), F32)], axis=0).astype(BF)
                acc = acc + dot_nt(signs.astype(F32).astype(BF), rhs)
        cols = jnp.where(lane == 0, gterm, jnp.where(lane == 1, bterm, 0.0))
        gb = jnp.transpose(jnp.concatenate([cols, jnp.zeros((96, 128), F32)], axis=0))
        e = acc[16:24] + pltpu.roll(gb[0:8], 2, 0)
        sm[...] = acc[0:8] + pltpu.roll(acc[8:16], 32, 1) + pltpu.roll(e, 64, 1)
        xb[x] = sm[...]
        for k in (2, 1, 3):
            send(("m1", k), sm, xb.at[x], "dp", ((x + k) % 4) * 4 + l)

    def m2():
        for k in (1, 2, 3):
            got(("m1", k), xb.at[(x + 4 - k) % 4])
        zb[l] = (xb[0] + xb[1]) + (xb[2] + xb[3])
        for k in (3, 2, 1):
            send(("m2", k), zb.at[l], zb.at[l], "dp", x * 4 + (l + k) % 4)

    def m3():
        for k in (1, 2, 3):
            got(("m2", k), zb.at[(l + 4 - k) % 4])
        smo[me] = (zb[0] + zb[1]) + (zb[2] + zb[3])
        for d in range(1, NS):
            send(("m3", d), smo.at[me], smo.at[me], "shard", (me + d) % NS)

    def m4():
        for d in range(1, NS):
            got(("m3", d), smo.at[(me + NS - d) % NS])

    ev = [(0.1, 0, first_out, (0, lambda t: act[t], 0, T)), (8.2, 0, second_out, (0, dec, 0, T))]
    for i, t in enumerate(order):
        ev += [
            (2.4 + 1.1 * i, 1, g_near, (t,)), (5.5 + 1.6 * i, 2, g_over, (t,)),
            (8.5 + 1.6 * i, 3, g_far, (t,)), (11.0 + 2.1 * i, 4, g_done, (t,)),
            (11.0 + 2.1 * i, 5, wgrad, (t,)), (11.1 + 2.1 * i, 30, dgrad, (t,)),
            (13.2 + 2.1 * i, 7, dsum, (t,)),
        ]
    ready = (15.22, 15.24, 17.32, 17.34, 19.42, 19.44, 19.46)
    for g in range(G):
        at = ready[g]
        lag = max(0.0, 15.3 + 1.0 * g - at)
        for off, n, f in ((0.0, 20, r1), (2.2, 21, r2), (4.6, 22, r3), (9.0, 23, r4), (13.0, 24, r5), (15.5, 25, r6), (18.0, 26, r7)):
            ev.append((at + off + (lag if off else 0.0), n, f, (g,)))
    get = lambda t: dft[t]
    ev += [
        (17.5, 30, first_out, (1, get, 2, T)), (20.6, 31, second_out, (1, gho, 2, T)),
        (21.7, 40, first_out, (1, get, 0, 2)), (21.8, 41, m1, ()),
        (25.3, 41, second_out, (1, gho, 0, 2)), (26.0, 42, m2, ()), (31.0, 43, m3, ()),
        (37.0, 45, m4, ()), (37.1, 46, third_out, (0, dec, 0, T)),
        (37.2, 47, third_out, (1, gho, 2, T)), (37.3, 48, third_out, (1, gho, 0, 2)),
    ]
    cw[6, 3] = jnp.zeros((4, 16, 256), BF)
    run(ev)
    for g in range(G):
        got(("r14", g), fin.at[g, :, :, :, other])
    wires.finish()


def block(lengths, ci, hid, emb, w, gain, bias, cot):
    v = pltpu.VMEM
    piece = (16, 256)
    return pl.pallas_call(
        block_body,
        out_shape=(
            jax.ShapeDtypeStruct((4, 160, 128), BF),
            jax.ShapeDtypeStruct((4, 160, 128), BF),
            jax.ShapeDtypeStruct((G, 4, 2, 16, 512), BF),
            jax.ShapeDtypeStruct((NS, 8, 128), F32),
        ),
        in_specs=[pl.BlockSpec(memory_space=pltpu.SMEM)] + [VM] * 7, out_specs=(VM,) * 4,
        scratch_shapes=[
            v((128, 512), BF), v((160, 512), BF), v((4, 160, 128), BF), v((2, 128, 128), F32),
            v((NS, 8, 128), jnp.int32),
            v((8, 80, 128), BF), v((NS, 80, 128), BF),
            v((4, 160, 128), BF), v((4, 160, 128), BF), v((4, 160, 128), BF),
            v((27, 2, 32, 256), BF), v((3, 256, 576), BF),
            v((T, 576, LP), BF), v((2, 4, T, 32, LP), BF),
            v((2, T, 2, 16, LP), BF), v((2, T, 2, 32, LP), BF), v((2, T, 2, 32, LP), BF),
            v((T, 32, LP), BF), v((T, 32, LP), BF), v((T, 32, LP), F32),
            v((T, 32, LP), F32), v((T, 32, LP), F32), v((T, 32, LP), F32), v((T, 32, LP), F32),
            v((T, 32, LP), BF), v((2, 4, T, 32, LP), BF), v((3, 576, 256), F32),
            v((G, 4, 4) + piece, BF),
            v((2, T, 32, LP), F32), v((2, T, 32, LP), BF), v((T, 32, LP), BF), v((T, 32, LP), F32),
            v((2, 4, 160, 128), BF), v((2, 4, 160, 128), BF), v((2, 4, 160, 128), BF),
            v((G, 4, 4) + piece, BF), v((2, G, 2) + piece, BF), v((2, G, 4) + piece, BF),
            v((2, G, 4) + piece, BF), v((G, 4) + piece, BF), v((G, 4) + piece, BF),
            v((8, 128), F32), v((4, 8, 128), F32), v((4, 8, 128), F32),
            pltpu.SemaphoreType.DMA((N_WIRES,)), pltpu.SemaphoreType.DMA((N_WIRES,)),
        ],
        compiler_params=params(0), name="block",
    )(lengths, ci, hid, emb, w, gain, bias, cot)


def outputs_body(dec, gho, fin, smo, dec_o, gh_o, gc_o, ge_o, gg_o, gb_o):
    lane = lax.broadcasted_iota(jnp.int32, (1, 128), 1)
    grp = [(lane // 32 == g).astype(F32) for g in range(4)]

    def gathered(parts):
        acc = None
        for g, (v, q) in enumerate(parts):
            v = v.astype(F32)
            v = v if g == q else pltpu.roll(v, (32 * (g - q)) % 128, 1)
            acc = v * grp[g] if acc is None else acc + v * grp[g]
        return acc

    for tap in range(27):
        gc_o[tap] = fin[tap // 4, tap % 4].reshape(32, 512).astype(F32)
    back = placing(1)
    for t in range(T):
        rows = slice(32 * t, 32 * t + 32)
        v = jnp.concatenate([dec[0, rows], dec[2, rows], dec[1, rows], dec[3, rows]], axis=0)
        dec_o[128 * t:128 * t + 128] = dot(back, v).astype(BF)
    for zz in range(2):
        for h in range(2):
            col = 2 * zz + h
            gh_o[:, 128 * col:128 * (col + 1)] = gathered(
                [(gho[2 * zz + g % 2], 2 * h + g // 2) for g in range(4)]
            ).astype(BF)
    for q in range(4):
        cols = slice(128 * q, 128 * (q + 1))
        for a in range(3):
            v = gathered([(smo[4 * q + j], a) for j in range(4)])
            n = min(8, CODE_BITS - 8 * a)
            ge_o[8 * a:8 * a + n, cols] = v[0:n]
        v = gathered([(smo[sid(q % 2, j, q // 2)], 2) for j in range(4)])
        gg_o[q:q + 1] = v[2:3]
        gb_o[q:q + 1] = v[3:4]


def outputs(dec, gho, fin, smo):
    s = jax.ShapeDtypeStruct
    return pl.pallas_call(
        outputs_body,
        out_shape=(
            s((640, 128), BF), s((160, 512), BF), s((27, 32, 512), F32), s((CODE_BITS, 512), F32),
            s((4, 128), F32), s((4, 128), F32),
        ),
        in_specs=[VM] * 4, out_specs=(VM,) * 6, compiler_params=params(), name="outputs",
    )(dec, gho, fin, smo)


def on_device(codes, lengths, hidden, embed, conv_weight, gain, bias, cotangent):
    ci = jnp.pad(codes.reshape(160), (0, 864)).reshape(8, 128)
    raw = block(
        lengths, ci, hidden.reshape(160, 512), embed, conv_weight.transpose(1, 0, 2),
        gain.reshape(4, 128), bias.reshape(4, 128), cotangent.reshape(640, 128),
    )
    dec, gh, gc, ge, gg, gb = outputs(*raw)
    return (
        dec.reshape(1, T, 2 * R, 2 * WD, 128), gh.reshape(1, T, R, WD, 512), gc.transpose(1, 0, 2), ge,
        gg.reshape(512), gb.reshape(512),
    )


def solution(mesh):
    return jax.shard_map(
        on_device,
        mesh=mesh,
        in_specs=(
            P("dp", None, None, "shard"),
            P("dp"),
            P("dp", None, None, "shard", None),
            P(),
            P("shard", None, None),
            P(),
            P(),
            P("dp", None, None, "shard", None),
        ),
        out_specs=(
            P("dp", None, None, "shard", None),
            P("dp", None, None, "shard", None),
            P("shard", None, None),
            P(),
            P(),
            P(),
        ),
        check_vma=False,
    )
```

```python
import jax
import jax.numpy as jnp
from jax import lax
from jax.experimental import pallas as pl
from jax.experimental.pallas import tpu as pltpu
from jax.sharding import PartitionSpec as P

BF = jnp.bfloat16
F32 = jnp.float32
CODE_BITS = 18
EPS = 1e-05
T = 5
R = 8
WD = 4
NS = 16
LP = 512
G = 7
MESH = pl.DeviceIdType.MESH
OFF_R = (0.0, 2.2, 4.6, 9.0, 13.0, 15.5, 18.0)
OFF_D = (0.0, 0.1, 3.4, 7.4, 11.4, 11.5, 15.0)
LAG = 1.0
TAIL = (17.5, 20.6, 21.7, 21.8, 25.3, 26.0, 31.0)
VM = pl.BlockSpec(memory_space=pltpu.VMEM)


def params(cid=None):
    if cid is None:
        return pltpu.CompilerParams(vmem_limit_bytes=60 * 1024 * 1024)
    return pltpu.CompilerParams(
        vmem_limit_bytes=60 * 1024 * 1024, collective_id=cid, has_side_effects=True
    )


def shard_spot():
    me = lax.axis_index("shard")
    return me, me // 8, (me // 2) % 4, me % 2


def sid(z, y, c):
    return z * 8 + y * 2 + c


def rcopy(src, dst, ssem, rsem, axis, peer):
    return pltpu.make_async_remote_copy(
        src_ref=src, dst_ref=dst, send_sem=ssem, recv_sem=rsem,
        device_id={axis: peer}, device_id_type=MESH,
    )


def lane_masks():
    lane = lax.broadcasted_iota(jnp.int32, (1, LP), 1)
    row = (lane // 4) % 8
    col = lane % 4
    return {
        "r0": row >= 1, "r2": row <= 6,
        "c0": col >= 1, "c2": col <= 2,
        "w0": lane % 4 + lane // 32 > 0, "w2": lane % 4 + 4 * (lane // 32) < 63,
    }


def row_shift(x, d, m):
    if d < 0:
        return jnp.where(m["r0"], pltpu.roll(x, 4, 1), 0.0)
    if d > 0:
        return jnp.where(m["r2"], pltpu.roll(x, LP - 4, 1), 0.0)
    return x


def col_shift(x, d, m):
    if d < 0:
        y = jnp.where(m["c0"], pltpu.roll(x, 1, 1), pltpu.roll(x, 29, 1))
        return jnp.where(m["w0"], y, 0.0)
    if d > 0:
        y = jnp.where(m["c2"], pltpu.roll(x, LP - 1, 1), pltpu.roll(x, LP - 29, 1))
        return jnp.where(m["w2"], y, 0.0)
    return x


def dot(a, b):
    return lax.dot_general(a, b, (((1,), (0,)), ((), ())), preferred_element_type=F32)


def dot_nt(a, b):
    return lax.dot_general(a, b, (((1,), (1,)), ((), ())), preferred_element_type=F32)


class Wires:
    def __init__(self, ss, rs):
        self.ss, self.rs, self.ids, self.started = ss, rs, {}, []

    def make(self, name, src, dst, axis, peer):
        n = self.ids.setdefault(name, len(self.ids))
        return rcopy(src, dst, self.ss.at[n], self.rs.at[n], axis, peer)

    def send(self, name, src, dst, axis, peer):
        cp = self.make(name, src, dst, axis, peer)
        cp.start()
        self.started.append(cp)

    def got(self, name, ref):
        self.make(name, ref, ref, "shard", (lax.axis_index("shard") + 1) % NS).wait_recv()

    def finish(self):
        for cp in self.started:
            cp.wait_send()


N_WIRES = 280
DIRECT = tuple(range(7))


def group_sum(x):
    s = jnp.sum(x, axis=1, keepdims=True)
    g = jnp.sum(s.reshape(2, 16, 1), axis=1, keepdims=True)
    return jnp.broadcast_to(g, (2, 16, 1)).reshape(32, 1)


def picks(rows, period):
    ch = lax.broadcasted_iota(jnp.int32, (rows, 128), 0)
    lane = lax.broadcasted_iota(jnp.int32, (rows, 128), 1)
    return (lane % period == ch).astype(F32).astype(BF)


def placing(way):
    dst = lax.broadcasted_iota(jnp.int32, (128, 128), way)
    src = lax.broadcasted_iota(jnp.int32, (128, 128), 1 - way)
    a, b, r, w = dst // 64, (dst // 32) % 2, (dst // 4) % 8, dst % 4
    return (src == 16 * r + 8 * a + 2 * w + b).astype(F32).astype(BF)


def block_body(
    length_ref, codes, hid, emb_ref, w, gain_ref, bias_ref, cot,
    dec, gho, fin, smo,
    ci, epad, fe, up, gcol, cbuf, fsrc, fbuf, u1, u2s, u2, w2s, wts, pat, part, rx1, tx2, rx2, txz, rxz, conv,
    ut, nrm, dpr, act, own, dcs, wacc, cw, df, db, drx, dft, d1s, d1, d2s,
    out, qx1, qt2, qx2, sx, rz, sm, xb, zb, ss, rs,
):
    me, z, y, c = shard_spot()
    dp = lax.axis_index("dp")
    x, l = dp // 4, dp % 4
    o = 1 - z
    yp, ym, far = (y + 1) % 4, (y + 3) % 4, (y + 2) % 4
    up_id, down_id, over, pair = sid(z, yp, c), sid(z, ym, c), sid(o, y, c), sid(z, y, 1 - c)
    xp, xm, xf = (x + 1) % 4, (x + 3) % 4, (x + 2) % 4
    fwd, bwd = xp * 4 + l, xm * 4 + l
    wires = Wires(ss, rs)
    send, got = wires.send, wires.got
    m = lane_masks()
    lane = lax.broadcasted_iota(jnp.int32, (1, 128), 1)
    grp = [(lane // 32 == g).astype(F32) for g in range(4)]
    grpb = [v.astype(BF) for v in grp]
    half = [(lane // 64 == g).astype(F32) for g in range(2)]
    halfb = [v.astype(BF) for v in half]

    barrier_sem = pltpu.get_barrier_semaphore()
    peers = [("shard", (me + d) % NS) for d in range(1, NS)]
    peers += [("dp", ((x + k) % 4) * 4 + l) for k in range(1, 4)]
    peers += [("dp", x * 4 + (l + k) % 4) for k in range(1, 4)]
    for axis, peer in peers:
        pl.semaphore_signal(barrier_sem, inc=1, device_id={axis: peer}, device_id_type=MESH)

    length = length_ref[0]
    mk = [jnp.where(t < length, 1.0, 0.0) for t in range(T)]
    slot = lax.broadcasted_iota(jnp.int32, (WD, 128), 1)
    column = lax.broadcasted_iota(jnp.int32, (WD, 128), 0)
    ci[...] = jnp.zeros((8, 128), jnp.int32)
    for h in range(2):
        v = jnp.zeros((WD, 128), jnp.int32)
        for t in range(4 * h, min(T, 4 * h + 4)):
            for r in range(R):
                one = jnp.broadcast_to(codes[t, :, r:r + 1], (WD, 128))
                v = jnp.where(slot // 4 == 8 * (t - 4 * h) + r, one, v)
        ci[h:h + 1, :] = jnp.sum(jnp.where(slot % 4 == column, v, 0), axis=0, keepdims=True)
    bit = lax.broadcasted_iota(jnp.int32, (128, 128), 0)
    epad[...] = jnp.zeros((128, 512), BF)
    epad[0:CODE_BITS] = emb_ref[...]
    for h in range(2):
        code = jnp.broadcast_to(ci[h:h + 1, :], (128, 128))
        signs = jnp.where(bit < CODE_BITS, (lax.shift_right_logical(code, jnp.minimum(bit, 31)) & 1) * 2 - 1, 0)
        nat = dot(jnp.transpose(signs.astype(F32)).astype(BF), epad[...])
        for t in range(4 * h, min(T, 4 * h + 4)):
            r0 = 32 * (t - 4 * h)
            fe[32 * t:32 * t + 32] = (
                (nat[r0:r0 + 32] + hid[t].astype(F32).reshape(32, 512)) * mk[t]
            ).astype(BF)
    place = placing(0)
    for t in range(T):
        v = dot(place, cot[128 * t:128 * t + 128]).astype(BF)
        for q in range(4):
            up[q, 32 * t:32 * t + 32] = v[32 * q:32 * q + 32]
    for k, ref in enumerate((gain_ref, bias_ref)):
        gcol[k] = jnp.transpose(jnp.broadcast_to(ref[pl.ds(2 * c + z, 1), :], (128, 128)))

    for col in range(4):
        a = fe[0:80, 128 * col:128 * (col + 1)].astype(F32)
        b = fe[80:160, 128 * col:128 * (col + 1)].astype(F32)
        fsrc[2 * col] = (a * half[0] + pltpu.roll(b, 64, 1) * half[1]).astype(BF)
        fsrc[2 * col + 1] = (pltpu.roll(a, 64, 1) * half[0] + b * half[1]).astype(BF)
    chip = 4 * z + y
    fbuf[me] = fsrc[chip]
    u1[2 * z + c] = up[2 * c + z]
    cbuf[me] = ci[...]
    pl.semaphore_wait(barrier_sem, len(peers))

    steps = [(0, 1), (0, 3), (1, 0), (0, 2), (1, 1), (1, 3), (1, 2)]
    for dz, dy in steps:
        zz, yy = (z + dz) % 2, (y + dy) % 4
        send(("f", dz, dy), fsrc.at[4 * zz + yy], fbuf.at[me], "shard", sid(zz, yy, c))
    send("fp", fbuf.at[me], fbuf.at[me], "shard", pair)
    send("w", w.at[:, :, pl.ds(pl.multiple_of(256 * (1 - c), 256), 256)], w2s.at[:, c], "shard", pair)
    w2s[:, c] = w[:, :, pl.ds(pl.multiple_of(256 * c, 256), 256)]

    def relay(dz, dy):
        frm = sid((z + dz) % 2, (y + 4 - dy) % 4, c)
        got(("f", dz, dy), fbuf.at[frm])
        send(("fr", dz, dy), fbuf.at[frm], fbuf.at[frm], "shard", pair)

    relay(0, 1)
    relay(0, 3)
    got("w", w2s.at[:, 1 - c])
    for dt in range(3):
        wts[dt] = jnp.transpose(w2s[9 * dt:9 * dt + 9].reshape(576, 256).astype(F32)).astype(BF)
    for dz, dy in steps[2:]:
        relay(dz, dy)
    got("fp", fbuf.at[pair])
    trio = [(0, 1), (1, 0), (1, 1)]
    for dz, dc in trio:
        zz, cc = (z + dz) % 2, (c + dc) % 2
        send(("u1", dz, dc), up.at[2 * cc + zz], u1.at[2 * z + c], "shard", sid(zz, y, cc))
    for d in range(1, NS):
        send(("b", d), ci, cbuf.at[me], "shard", (me + d) % NS)
    for dz, dy in steps:
        got(("fr", dz, dy), fbuf.at[sid((z + dz) % 2, (y + 4 - dy) % 4, 1 - c)])

    sel64, sel32 = picks(64, 64), picks(32, 32)

    def features(t):
        pieces = []
        for h in range(2):
            p = 32 * t + 16 * h
            k = p // 80
            p = p - 80 * k
            pieces.append(fbuf[:, p:p + 16, :] * halfb[k][None])
        rows = jnp.concatenate(pieces, axis=1).reshape(LP, 128)
        f = dot_nt(sel64, rows)
        for dw in range(3):
            fc = col_shift(f, dw - 1, m)
            for dr in range(3):
                k = 3 * dr + dw
                pat[t, 64 * k:64 * (k + 1), :] = row_shift(fc, dr - 1, m).astype(BF)

    def comp(t):
        features(t)
        acc = None
        for dt in range(3):
            if t - 2 + dt >= 0:
                d = dot(wts[dt], pat[t - 2 + dt])
                acc = d if acc is None else acc + d
        for k in range(8):
            part[k // 4, k % 4, t] = acc[32 * k:32 * (k + 1)].astype(BF)
        send(("s1a", t), part.at[:, far, t, pl.ds(0, 16)], rx1.at[0, t], "shard", up_id)
        send(("s1b", t), part.at[:, far, t, pl.ds(16, 16)], rx1.at[1, t], "shard", down_id)

    def s2(t):
        got(("s1a", t), rx1.at[0, t])
        tx2[0, t, :, 0:16] = (part[:, yp, t, 0:16].astype(F32) + rx1[0, t].astype(F32)).astype(BF)
        tx2[0, t, :, 16:32] = part[:, yp, t, 16:32]
        send(("s2a", t), tx2.at[0, t], rx2.at[0, t], "shard", up_id)
        got(("s1b", t), rx1.at[1, t])
        tx2[1, t, :, 16:32] = (part[:, ym, t, 16:32].astype(F32) + rx1[1, t].astype(F32)).astype(BF)
        tx2[1, t, :, 0:16] = part[:, ym, t, 0:16]
        send(("s2b", t), tx2.at[1, t], rx2.at[1, t], "shard", down_id)

    def s3(t):
        got(("s2a", t), rx2.at[0, t])
        got(("s2b", t), rx2.at[1, t])
        txz[t] = (
            part[o, y, t].astype(F32) + rx2[0, t, o].astype(F32) + rx2[1, t, o].astype(F32)
        ).astype(BF)
        send(("s3", t), txz.at[t], rxz.at[t], "shard", over)
        conv[t] = part[z, y, t].astype(F32) + rx2[0, t, z].astype(F32) + rx2[1, t, z].astype(F32)

    def s4(t):
        got(("s3", t), rxz.at[t])
        conv[t] = conv[t] + rxz[t].astype(F32)

    def u_second():
        for dz, dc in trio:
            zz, cc = (z + dz) % 2, (c + dc) % 2
            got(("u1", dz, dc), u1.at[2 * zz + cc])
        for q in range(4):
            acc = None
            for g in range(4):
                v = u1[g].astype(F32)
                v = v if g == q else pltpu.roll(v, (32 * (g - q)) % 128, 1)
                acc = v * grp[g] if acc is None else acc + v * grp[g]
            u2s[q] = acc.astype(BF)
        for dy in (1, 3, 2):
            yy = (y + dy) % 4
            send(("u2", dy), u2s.at[yy], u2.at[y], "shard", sid(z, yy, c))
        u2[y] = u2s[y]

    def u_third():
        for dy in (1, 3, 2):
            got(("u2", dy), u2.at[(y + 4 - dy) % 4])
        for t in range(T):
            blocks = []
            for s in range(NS):
                blocks.append(u2[(s // 2) % 4, 32 * t:32 * t + 32, :] * grpb[2 * (s // 8) + s % 2])
            ut[t] = dot_nt(sel32, jnp.concatenate(blocks, axis=0))

    def run(events):
        for _, _, f, args in sorted(events, key=lambda e: e[:2]):
            f(*args)

    ev = []
    for t in range(T):
        ev += [
            (1.5 * t, 0, comp, (t,)), (2.6 + 2.1 * t, 1, s2, (t,)),
            (5.2 + 2.1 * t, 2, s3, (t,)), (11.0 + 2.1 * t, 3, s4, (t,)),
        ]
    ev += [(7.0, 9, u_second, ()), (14.5, 9, u_third, ())]
    run(ev)

    count = length.astype(F32) * float(R * WD * NS * 16)
    s_one = jnp.zeros((32, LP), F32)
    s_two = jnp.zeros((32, LP), F32)
    for t in range(T):
        v = conv[t] * mk[t]
        s_one = s_one + v
        s_two = s_two + conv[t] * v
    mean = group_sum(s_one) / count
    inv = lax.rsqrt(group_sum(s_two) / count - mean * mean + EPS)
    mine32 = pl.ds(pl.multiple_of(32 * y, 32), 32)
    gain, bias = gcol[0, mine32, 0:1], gcol[1, mine32, 0:1]
    a1 = jnp.zeros((32, LP), F32)
    a2 = jnp.zeros((32, LP), F32)
    for t in range(T):
        n = (conv[t] - mean) * inv
        pre = n * gain + bias
        sg = jax.nn.sigmoid(pre)
        act[t] = pre * sg * mk[t]
        d = ut[t] * mk[t] * sg * (1.0 + pre * (1.0 - sg))
        a1 = a1 + d
        a2 = a2 + d * n
        nrm[t] = n
        dpr[t] = d
    bterm = jnp.sum(a1, axis=1, keepdims=True)
    gterm = jnp.sum(a2, axis=1, keepdims=True)
    t1 = group_sum(gain * bterm) / count
    t2 = group_sum(gain * gterm) / count

    lo, hi = pl.ds(0, 16), pl.ds(16, 16)
    order = [4, 3, 2, 1, 0]
    for t in order:
        own[t] = (inv * (dpr[t] * gain - t1 - nrm[t] * t2) * mk[t]).astype(BF)
        send(("g0", t), own.at[t], dcs.at[z, y, t], "shard", over)
        send(("g1", t), own.at[t], dcs.at[z, y, t], "shard", up_id)
        send(("g2", t), own.at[t], dcs.at[z, y, t], "shard", down_id)
    for t in order:
        dcs[z, y, t] = own[t]

    def first_out(kind, get, t0, t1):
        pack_out(kind, get, t0, t1)
        send_out(kind, t0, t1)

    def pack_out(kind, get, t0, t1):
        for t in range(t0, t1):
            v = get(t)
            nat = jnp.transpose(jnp.concatenate([v, v, v, v], axis=0))
            for q in range(4):
                acc = None
                for g in range(4):
                    r0 = 32 * sid(g // 2, q, g % 2)
                    piece = nat[r0:r0 + 32] * grp[g]
                    acc = piece if acc is None else acc + piece
                d1s[kind, q, 32 * t:32 * t + 32, :] = acc.astype(BF)

    def send_out(kind, t0, t1):
        for dy in (1, 3, 2):
            yy = (y + dy) % 4
            part_of = pl.ds(32 * t0, 32 * (t1 - t0))
            send(
                ("d1", kind, t0, dy), d1s.at[kind, yy, part_of], d1.at[kind, y, part_of], "shard", sid(z, yy, c)
            )
        d1[kind, y, 32 * t0:32 * t1] = d1s[kind, y, 32 * t0:32 * t1]

    def second_out(kind, dst, t0, t1):
        part_of = pl.ds(32 * t0, 32 * (t1 - t0))
        for dy in (1, 3, 2):
            got(("d1", kind, t0, dy), d1.at[kind, (y + 4 - dy) % 4, part_of])
        for g in range(4):
            acc = None
            for q in range(4):
                v = d1[kind, q, 32 * t0:32 * t1].astype(F32)
                v = v if g == q else pltpu.roll(v, (32 * (q - g)) % 128, 1)
                acc = v * grp[q] if acc is None else acc + v * grp[q]
            d2s[kind, g, 32 * t0:32 * t1] = acc.astype(BF)
        for dz, dc in trio:
            zz, cc = (z + dz) % 2, (c + dc) % 2
            send(
                ("d2", kind, t0, dz, dc), d2s.at[kind, 2 * zz + cc, part_of], dst.at[2 * z + c, part_of],
                "shard", sid(zz, y, cc),
            )
        dst[2 * z + c, 32 * t0:32 * t1] = d2s[kind, 2 * z + c, 32 * t0:32 * t1]

    def third_out(kind, dst, t0, t1):
        part_of = pl.ds(32 * t0, 32 * (t1 - t0))
        for dz, dc in trio:
            got(("d2", kind, t0, dz, dc), dst.at[2 * ((z + dz) % 2) + (c + dc) % 2, part_of])

    def g_near(t):
        got(("g1", t), dcs.at[z, ym, t])
        send(("g3", t), dcs.at[z, ym, t, lo], dcs.at[z, ym, t, lo], "shard", up_id)
        got(("g2", t), dcs.at[z, yp, t])
        send(("g4", t), dcs.at[z, yp, t, hi], dcs.at[z, yp, t, hi], "shard", down_id)

    def g_over(t):
        got(("g0", t), dcs.at[o, y, t])
        send(("g5", t), dcs.at[o, y, t], dcs.at[o, y, t], "shard", up_id)
        send(("g6", t), dcs.at[o, y, t], dcs.at[o, y, t], "shard", down_id)

    def g_far(t):
        got(("g5", t), dcs.at[o, ym, t])
        send(("g7", t), dcs.at[o, ym, t, lo], dcs.at[o, ym, t, lo], "shard", up_id)
        got(("g6", t), dcs.at[o, yp, t])
        send(("g8", t), dcs.at[o, yp, t, hi], dcs.at[o, yp, t, hi], "shard", down_id)

    def g_done(t):
        got(("g3", t), dcs.at[z, far, t, lo])
        got(("g4", t), dcs.at[z, far, t, hi])
        got(("g7", t), dcs.at[o, far, t, lo])
        got(("g8", t), dcs.at[o, far, t, hi])

    def dgrad(t):
        acc = None
        for dt in range(3):
            if t + 2 - dt < T:
                d = dot(w2s[9 * dt:9 * dt + 9].reshape(576, 256), dcs[:, :, t + 2 - dt].reshape(256, LP))
                acc = d if acc is None else acc + d
        total = None
        for dw in range(3):
            rows = None
            for dr in range(3):
                k = 3 * dr + dw
                s = row_shift(acc[64 * k:64 * (k + 1)], 1 - dr, m)
                rows = s if rows is None else rows + s
            s = col_shift(rows, 1 - dw, m)
            total = s if total is None else total + s
        for h in range(2):
            df[h, t] = total[32 * h:32 * (h + 1)]
            db[h, t] = total[32 * h:32 * (h + 1)].astype(BF)
        send(("pair", t), db.at[1 - c, t], drx.at[t], "shard", pair)

    def wgrad(t):
        dct = dcs[:, :, t].reshape(256, LP)
        for dt in range(3):
            if t - 2 + dt < 0:
                continue
            v = dot_nt(pat[t - 2 + dt], dct)
            if t < T - 1:
                v = v + wacc[dt]
            if t == 2 - dt:
                for k in range(9):
                    tap = 9 * dt + k
                    cw[tap // 4, tap % 4] = v[64 * k:64 * (k + 1)].astype(BF).reshape(4, 16, 256)
            else:
                wacc[dt] = v

    def dsum(t):
        got(("pair", t), drx.at[t])
        dft[t] = (df[c, t] + drx[t].astype(F32)).astype(BF).astype(F32) * mk[t]

    lo4, hi4 = pl.ds(0, 2), pl.ds(2, 2)

    xfar = xf * 4 + l

    def r1(g):
        if g in DIRECT:
            send(("r15", g), cw.at[g, xf], qx2.at[2, g], "dp", xfar)
            send(("r2", g), cw.at[g, xp], qx2.at[0, g], "dp", fwd)
            send(("r3", g), cw.at[g, xm], qx2.at[1, g], "dp", bwd)
            return
        send(("r0", g), cw.at[g, xf, lo4], qx1.at[0, g], "dp", fwd)
        send(("r1", g), cw.at[g, xf, hi4], qx1.at[1, g], "dp", bwd)

    def r2(g):
        if g in DIRECT:
            return
        got(("r0", g), qx1.at[0, g])
        qt2[0, g, 0:2] = (cw[g, xp, 0:2].astype(F32) + qx1[0, g].astype(F32)).astype(BF)
        qt2[0, g, 2:4] = cw[g, xp, 2:4]
        send(("r2", g), qt2.at[0, g], qx2.at[0, g], "dp", fwd)
        got(("r1", g), qx1.at[1, g])
        qt2[1, g, 2:4] = (cw[g, xm, 2:4].astype(F32) + qx1[1, g].astype(F32)).astype(BF)
        qt2[1, g, 0:2] = cw[g, xm, 0:2]
        send(("r3", g), qt2.at[1, g], qx2.at[1, g], "dp", bwd)

    def r3(g):
        got(("r2", g), qx2.at[0, g])
        got(("r3", g), qx2.at[1, g])
        tot = cw[g, x].astype(F32) + qx2[0, g].astype(F32) + qx2[1, g].astype(F32)
        if g in DIRECT:
            got(("r15", g), qx2.at[2, g])
            tot = tot + qx2[2, g].astype(F32)
        sx[g] = tot.astype(BF)
        for k in (3, 2, 1):
            send(("r4", k, g), sx.at[g, (l + k) % 4], rz.at[g, k], "dp", x * 4 + (l + k) % 4)

    def r4(g):
        tot = sx[g, l].astype(F32)
        for k in (1, 2, 3):
            got(("r4", k, g), rz.at[g, k])
            tot = tot + rz[g, k].astype(F32)
        out[g, x, l] = tot.astype(BF)
        for k in (3, 2, 1):
            send(("r7", k, g), out.at[g, x, l], out.at[g, x, l], "dp", x * 4 + (l + k) % 4)

    def r5(g):
        for k in (1, 2, 3):
            got(("r7", k, g), out.at[g, x, (l + 4 - k) % 4])
        send(("r10", g), out.at[g, x], out.at[g, x], "dp", fwd)
        send(("r11", g), out.at[g, x], out.at[g, x], "dp", bwd)
        if g in DIRECT:
            send(("r16", g), out.at[g, x], out.at[g, x], "dp", xfar)

    def r6(g):
        if g in DIRECT:
            return
        got(("r10", g), out.at[g, xm])
        send(("r12", g), out.at[g, xm, lo4], out.at[g, xm, lo4], "dp", fwd)
        got(("r11", g), out.at[g, xp])
        send(("r13", g), out.at[g, xp, hi4], out.at[g, xp, hi4], "dp", bwd)

    mine = pl.ds(pl.multiple_of(256 * c, 256), 256)
    other = pl.ds(pl.multiple_of(256 * (1 - c), 256), 256)

    def r7(g):
        if g in DIRECT:
            got(("r10", g), out.at[g, xm])
            got(("r11", g), out.at[g, xp])
            got(("r16", g), out.at[g, xf])
        else:
            got(("r12", g), out.at[g, xf, lo4])
            got(("r13", g), out.at[g, xf, hi4])
        send(("r14", g), out.at[g, :, pl.ds(2 * (1 - c), 2)], fin.at[g, :, :, :, mine], "shard", pair)
        fin[g, :, :, :, mine] = out[g, :, pl.ds(2 * c, 2)]

    def m1():
        for d in range(1, NS):
            got(("b", d), cbuf.at[(me + NS - d) % NS])
        grpi = [(lane // 32 == g).astype(jnp.int32) for g in range(4)]
        bit32 = lax.broadcasted_iota(jnp.int32, (32, LP), 0)
        acc = jnp.zeros((32, 128), F32)
        for f in range(4):
            cols = []
            for q in range(4):
                v = None
                for j in range(4):
                    r = cbuf[4 * q + j]
                    r = r if j == f else pltpu.roll(r, (32 * (j - f)) % 128, 1)
                    v = r * grpi[j] if v is None else v + r * grpi[j]
                cols.append(v)
            for t in ((0, 4) if f == 0 else (f,)):
                code = jnp.concatenate([v[t // 4:t // 4 + 1] for v in cols], axis=1)
                code = jnp.broadcast_to(code, (32, LP))
                signs = jnp.where(bit32 < CODE_BITS, (lax.shift_right_logical(code, bit32) & 1) * 2 - 1, 0)
                rhs = jnp.concatenate([dft[t], jnp.zeros((96, LP), F32)], axis=0).astype(BF)
                acc = acc + dot_nt(signs.astype(F32).astype(BF), rhs)
        cols = jnp.where(lane == 0, gterm, jnp.where(lane == 1, bterm, 0.0))
        gb = jnp.transpose(jnp.concatenate([cols, jnp.zeros((96, 128), F32)], axis=0))
        e = acc[16:24] + pltpu.roll(gb[0:8], 2, 0)
        sm[...] = acc[0:8] + pltpu.roll(acc[8:16], 32, 1) + pltpu.roll(e, 64, 1)
        xb[x] = sm[...]
        for k in (2, 1, 3):
            send(("m1", k), sm, xb.at[x], "dp", ((x + k) % 4) * 4 + l)

    def m2():
        for k in (1, 2, 3):
            got(("m1", k), xb.at[(x + 4 - k) % 4])
        zb[l] = (xb[0] + xb[1]) + (xb[2] + xb[3])
        for k in (3, 2, 1):
            send(("m2", k), zb.at[l], zb.at[l], "dp", x * 4 + (l + k) % 4)

    def m3():
        for k in (1, 2, 3):
            got(("m2", k), zb.at[(l + 4 - k) % 4])
        smo[me] = (zb[0] + zb[1]) + (zb[2] + zb[3])
        for d in range(1, NS):
            send(("m3", d), smo.at[me], smo.at[me], "shard", (me + d) % NS)

    def m4():
        for d in range(1, NS):
            got(("m3", d), smo.at[(me + NS - d) % NS])

    ev = [(2.3 + 1.1 * t, 0, pack_out, (0, lambda t: act[t], t, t + 1)) for t in range(T)]
    ev += [(7.6, 0, send_out, (0, 0, T)), (24.2, 0, second_out, (0, dec, 0, T))]
    for i, t in enumerate(order):
        ev += [
            (2.4 + 1.1 * i, 1, g_near, (t,)), (5.5 + 1.6 * i, 2, g_over, (t,)),
            (8.5 + 1.6 * i, 3, g_far, (t,)), (11.0 + 2.1 * i, 4, g_done, (t,)),
            (11.0 + 2.1 * i, 5, wgrad, (t,)), (11.1 + 2.1 * i, 30, dgrad, (t,)),
            (13.2 + 2.1 * i, 7, dsum, (t,)),
        ]
    ready = (15.22, 15.24, 17.32, 17.34, 19.42, 19.44, 19.46)
    for g in range(G):
        at = ready[g]
        lag = max(0.0, 15.3 + LAG * g - at)
        offs = OFF_D if g in DIRECT else OFF_R
        for off, n, f in zip(offs, range(20, 27), (r1, r2, r3, r4, r5, r6, r7)):
            ev.append((at + off + (lag if off else 0.0), n, f, (g,)))
    get = lambda t: dft[t]
    ev += [
        (TAIL[0], 30, first_out, (1, get, 2, T)), (TAIL[1], 31, second_out, (1, gho, 2, T)),
        (TAIL[2], 40, first_out, (1, get, 0, 2)), (TAIL[3], 41, m1, ()),
        (TAIL[4], 41, second_out, (1, gho, 0, 2)), (TAIL[5], 42, m2, ()), (TAIL[6], 43, m3, ()),
        (37.0, 45, m4, ()), (37.1, 46, third_out, (0, dec, 0, T)),
        (37.2, 47, third_out, (1, gho, 2, T)), (37.3, 48, third_out, (1, gho, 0, 2)),
    ]
    cw[6, 3] = jnp.zeros((4, 16, 256), BF)
    run(ev)
    for g in range(G):
        got(("r14", g), fin.at[g, :, :, :, other])
    wires.finish()


def block(lengths, codes, hid, emb, w, gain, bias, cot):
    v = pltpu.VMEM
    piece = (16, 256)
    return pl.pallas_call(
        block_body,
        out_shape=(
            jax.ShapeDtypeStruct((4, 160, 128), BF),
            jax.ShapeDtypeStruct((4, 160, 128), BF),
            jax.ShapeDtypeStruct((G, 4, 2, 16, 512), BF),
            jax.ShapeDtypeStruct((NS, 8, 128), F32),
        ),
        in_specs=[pl.BlockSpec(memory_space=pltpu.SMEM)] + [VM] * 7, out_specs=(VM,) * 4,
        scratch_shapes=[
            v((8, 128), jnp.int32),
            v((128, 512), BF), v((160, 512), BF), v((4, 160, 128), BF), v((2, 128, 128), F32),
            v((NS, 8, 128), jnp.int32),
            v((8, 80, 128), BF), v((NS, 80, 128), BF),
            v((4, 160, 128), BF), v((4, 160, 128), BF), v((4, 160, 128), BF),
            v((27, 2, 32, 256), BF), v((3, 256, 576), BF),
            v((T, 576, LP), BF), v((2, 4, T, 32, LP), BF),
            v((2, T, 2, 16, LP), BF), v((2, T, 2, 32, LP), BF), v((2, T, 2, 32, LP), BF),
            v((T, 32, LP), BF), v((T, 32, LP), BF), v((T, 32, LP), F32),
            v((T, 32, LP), F32), v((T, 32, LP), F32), v((T, 32, LP), F32), v((T, 32, LP), F32),
            v((T, 32, LP), BF), v((2, 4, T, 32, LP), BF), v((3, 576, 256), F32),
            v((G, 4, 4) + piece, BF),
            v((2, T, 32, LP), F32), v((2, T, 32, LP), BF), v((T, 32, LP), BF), v((T, 32, LP), F32),
            v((2, 4, 160, 128), BF), v((2, 4, 160, 128), BF), v((2, 4, 160, 128), BF),
            v((G, 4, 4) + piece, BF), v((2, G, 2) + piece, BF), v((2, G, 4) + piece, BF),
            v((3, G, 4) + piece, BF), v((G, 4) + piece, BF), v((G, 4) + piece, BF),
            v((8, 128), F32), v((4, 8, 128), F32), v((4, 8, 128), F32),
            pltpu.SemaphoreType.DMA((N_WIRES,)), pltpu.SemaphoreType.DMA((N_WIRES,)),
        ],
        compiler_params=params(0), name="block",
    )(lengths, codes, hid, emb, w, gain, bias, cot)


def outputs_body(dec, gho, fin, smo, dec_o, gh_o, gc_o, ge_o, gg_o, gb_o):
    lane = lax.broadcasted_iota(jnp.int32, (1, 128), 1)
    grp = [(lane // 32 == g).astype(F32) for g in range(4)]

    def gathered(parts):
        acc = None
        for g, (v, q) in enumerate(parts):
            v = v.astype(F32)
            v = v if g == q else pltpu.roll(v, (32 * (g - q)) % 128, 1)
            acc = v * grp[g] if acc is None else acc + v * grp[g]
        return acc

    for tap in range(27):
        gc_o[tap] = fin[tap // 4, tap % 4].reshape(32, 512).astype(F32)
    back = placing(1)
    for t in range(T):
        rows = slice(32 * t, 32 * t + 32)
        v = jnp.concatenate([dec[0, rows], dec[2, rows], dec[1, rows], dec[3, rows]], axis=0)
        dec_o[128 * t:128 * t + 128] = dot(back, v).astype(BF)
    for zz in range(2):
        for h in range(2):
            col = 2 * zz + h
            v = gathered([(gho[2 * zz + g % 2], 2 * h + g // 2) for g in range(4)])
            gh_o[:, :, :, 128 * col:128 * (col + 1)] = v.reshape(T, R, WD, 128).astype(BF)
    for q in range(4):
        cols = slice(128 * q, 128 * (q + 1))
        for a in range(3):
            v = gathered([(smo[4 * q + j], a) for j in range(4)])
            n = min(8, CODE_BITS - 8 * a)
            ge_o[8 * a:8 * a + n, cols] = v[0:n]
        v = gathered([(smo[sid(q % 2, j, q // 2)], 2) for j in range(4)])
        gg_o[q:q + 1] = v[2:3]
        gb_o[q:q + 1] = v[3:4]


def outputs(dec, gho, fin, smo):
    s = jax.ShapeDtypeStruct
    return pl.pallas_call(
        outputs_body,
        out_shape=(
            s((640, 128), BF), s((T, R, WD, 512), BF), s((27, 32, 512), F32), s((CODE_BITS, 512), F32),
            s((4, 128), F32), s((4, 128), F32),
        ),
        in_specs=[VM] * 4, out_specs=(VM,) * 6, compiler_params=params(), name="outputs",
    )(dec, gho, fin, smo)


def on_device(codes, lengths, hidden, embed, conv_weight, gain, bias, cotangent):
    raw = block(
        lengths, codes[0].transpose(0, 2, 1), hidden[0], embed, conv_weight.transpose(1, 0, 2),
        gain.reshape(4, 128), bias.reshape(4, 128), cotangent.reshape(640, 128),
    )
    dec, gh, gc, ge, gg, gb = outputs(*raw)
    return (
        dec.reshape(1, T, 2 * R, 2 * WD, 128), gh[None], gc.transpose(1, 0, 2), ge,
        gg.reshape(512), gb.reshape(512),
    )


def solution(mesh):
    return jax.shard_map(
        on_device,
        mesh=mesh,
        in_specs=(
            P("dp", None, None, "shard"),
            P("dp"),
            P("dp", None, None, "shard", None),
            P(),
            P("shard", None, None),
            P(),
            P(),
            P("dp", None, None, "shard", None),
        ),
        out_specs=(
            P("dp", None, None, "shard", None),
            P("dp", None, None, "shard", None),
            P("shard", None, None),
            P(),
            P(),
            P(),
        ),
        check_vma=False,
    )
```

```python
import jax
import jax.numpy as jnp
from jax import lax
from jax.experimental import pallas as pl
from jax.experimental.pallas import tpu as pltpu
from jax.sharding import PartitionSpec as P

BF = jnp.bfloat16
F32 = jnp.float32
CODE_BITS = 18
EPS = 1e-05
T = 5
R = 8
WD = 4
NS = 16
LP = 512
G = 7
MESH = pl.DeviceIdType.MESH
OFF_R = (0.0, 2.2, 4.6, 9.0, 13.0, 15.5, 18.0)
OFF_D = (0.0, 0.1, 3.4, 7.4, 11.4, 11.5, 15.0)
LAG = 1.0
TAIL = (17.5, 20.6, 21.7, 21.8, 25.3, 26.0, 31.0)
VM = pl.BlockSpec(memory_space=pltpu.VMEM)


def params(cid=None):
    if cid is None:
        return pltpu.CompilerParams(vmem_limit_bytes=60 * 1024 * 1024)
    return pltpu.CompilerParams(
        vmem_limit_bytes=60 * 1024 * 1024, collective_id=cid, has_side_effects=True
    )


def shard_spot():
    me = lax.axis_index("shard")
    return me, me // 8, (me // 2) % 4, me % 2


def sid(z, y, c):
    return z * 8 + y * 2 + c


def rcopy(src, dst, ssem, rsem, axis, peer):
    return pltpu.make_async_remote_copy(
        src_ref=src, dst_ref=dst, send_sem=ssem, recv_sem=rsem,
        device_id={axis: peer}, device_id_type=MESH,
    )


def lane_masks():
    lane = lax.broadcasted_iota(jnp.int32, (1, LP), 1)
    row = (lane // 4) % 8
    col = lane % 4
    return {
        "r0": row >= 1, "r2": row <= 6,
        "c0": col >= 1, "c2": col <= 2,
        "w0": lane % 4 + lane // 32 > 0, "w2": lane % 4 + 4 * (lane // 32) < 63,
    }


def row_shift(x, d, m):
    if d < 0:
        return jnp.where(m["r0"], pltpu.roll(x, 4, 1), 0.0)
    if d > 0:
        return jnp.where(m["r2"], pltpu.roll(x, LP - 4, 1), 0.0)
    return x


def col_shift(x, d, m):
    if d < 0:
        y = jnp.where(m["c0"], pltpu.roll(x, 1, 1), pltpu.roll(x, 29, 1))
        return jnp.where(m["w0"], y, 0.0)
    if d > 0:
        y = jnp.where(m["c2"], pltpu.roll(x, LP - 1, 1), pltpu.roll(x, LP - 29, 1))
        return jnp.where(m["w2"], y, 0.0)
    return x


def dot(a, b):
    return lax.dot_general(a, b, (((1,), (0,)), ((), ())), preferred_element_type=F32)


def dot_nt(a, b):
    return lax.dot_general(a, b, (((1,), (1,)), ((), ())), preferred_element_type=F32)


class Wires:
    def __init__(self, ss, rs):
        self.ss, self.rs, self.ids, self.started = ss, rs, {}, []

    def make(self, name, src, dst, axis, peer):
        n = self.ids.setdefault(name, len(self.ids))
        return rcopy(src, dst, self.ss.at[n], self.rs.at[n], axis, peer)

    def send(self, name, src, dst, axis, peer):
        cp = self.make(name, src, dst, axis, peer)
        cp.start()
        self.started.append(cp)

    def got(self, name, ref):
        self.make(name, ref, ref, "shard", (lax.axis_index("shard") + 1) % NS).wait_recv()

    def finish(self):
        for cp in self.started:
            cp.wait_send()


N_WIRES = 290
SCATTER_DIRECT = (0, 1, 2, 3, 4)
GATHER_DIRECT = (0, 1, 2, 3, 4)
DIRECT = tuple(range(7))


def group_sum(x):
    s = jnp.sum(x, axis=1, keepdims=True)
    g = jnp.sum(s.reshape(2, 16, 1), axis=1, keepdims=True)
    return jnp.broadcast_to(g, (2, 16, 1)).reshape(32, 1)


def picks(rows, period):
    ch = lax.broadcasted_iota(jnp.int32, (rows, 128), 0)
    lane = lax.broadcasted_iota(jnp.int32, (rows, 128), 1)
    return (lane % period == ch).astype(F32).astype(BF)


def placing(way):
    dst = lax.broadcasted_iota(jnp.int32, (128, 128), way)
    src = lax.broadcasted_iota(jnp.int32, (128, 128), 1 - way)
    a, b, r, w = dst // 64, (dst // 32) % 2, (dst // 4) % 8, dst % 4
    return (src == 16 * r + 8 * a + 2 * w + b).astype(F32).astype(BF)


def block_body(
    length_ref, codes, hid, emb_ref, w, gain_ref, bias_ref, cot,
    dec, gho, fin, smo,
    ci, epad, fe, up, gcol, cbuf, fsrc, fbuf, u1, u2s, u2, w2s, wts, pat, part, rx1, tx2, rx2, rxf, txz, rxz, conv,
    ut, nrm, dpr, act, own, dcs, wacc, cw, df, db, drx, dft, d1s, d1, d2s,
    out, qx1, qt2, qx2, sx, rz, sm, xb, zb, ss, rs,
):
    me, z, y, c = shard_spot()
    dp = lax.axis_index("dp")
    x, l = dp // 4, dp % 4
    o = 1 - z
    yp, ym, far = (y + 1) % 4, (y + 3) % 4, (y + 2) % 4
    far_id = sid(z, far, c)
    up_id, down_id, over, pair = sid(z, yp, c), sid(z, ym, c), sid(o, y, c), sid(z, y, 1 - c)
    xp, xm, xf = (x + 1) % 4, (x + 3) % 4, (x + 2) % 4
    fwd, bwd = xp * 4 + l, xm * 4 + l
    wires = Wires(ss, rs)
    send, got = wires.send, wires.got
    m = lane_masks()
    lane = lax.broadcasted_iota(jnp.int32, (1, 128), 1)
    grp = [(lane // 32 == g).astype(F32) for g in range(4)]
    grpb = [v.astype(BF) for v in grp]
    half = [(lane // 64 == g).astype(F32) for g in range(2)]
    halfb = [v.astype(BF) for v in half]

    barrier_sem = pltpu.get_barrier_semaphore()
    peers = [("shard", (me + d) % NS) for d in range(1, NS)]
    peers += [("dp", ((x + k) % 4) * 4 + l) for k in range(1, 4)]
    peers += [("dp", x * 4 + (l + k) % 4) for k in range(1, 4)]
    for axis, peer in peers:
        pl.semaphore_signal(barrier_sem, inc=1, device_id={axis: peer}, device_id_type=MESH)

    length = length_ref[0]
    mk = [jnp.where(t < length, 1.0, 0.0) for t in range(T)]
    slot = lax.broadcasted_iota(jnp.int32, (WD, 128), 1)
    column = lax.broadcasted_iota(jnp.int32, (WD, 128), 0)
    ci[...] = jnp.zeros((8, 128), jnp.int32)
    for h in range(2):
        v = jnp.zeros((WD, 128), jnp.int32)
        for t in range(4 * h, min(T, 4 * h + 4)):
            for r in range(R):
                one = jnp.broadcast_to(codes[t, :, r:r + 1], (WD, 128))
                v = jnp.where(slot // 4 == 8 * (t - 4 * h) + r, one, v)
        ci[h:h + 1, :] = jnp.sum(jnp.where(slot % 4 == column, v, 0), axis=0, keepdims=True)
    bit = lax.broadcasted_iota(jnp.int32, (128, 128), 0)
    epad[...] = jnp.zeros((128, 512), BF)
    epad[0:CODE_BITS] = emb_ref[...]
    for h in range(2):
        code = jnp.broadcast_to(ci[h:h + 1, :], (128, 128))
        signs = jnp.where(bit < CODE_BITS, (lax.shift_right_logical(code, jnp.minimum(bit, 31)) & 1) * 2 - 1, 0)
        nat = dot(jnp.transpose(signs.astype(F32)).astype(BF), epad[...])
        for t in range(4 * h, min(T, 4 * h + 4)):
            r0 = 32 * (t - 4 * h)
            fe[32 * t:32 * t + 32] = (
                (nat[r0:r0 + 32] + hid[t].astype(F32).reshape(32, 512)) * mk[t]
            ).astype(BF)
    place = placing(0)
    for t in range(T):
        v = dot(place, cot[128 * t:128 * t + 128]).astype(BF)
        for q in range(4):
            up[q, 32 * t:32 * t + 32] = v[32 * q:32 * q + 32]
    for k, ref in enumerate((gain_ref, bias_ref)):
        gcol[k] = jnp.transpose(jnp.broadcast_to(ref[pl.ds(2 * c + z, 1), :], (128, 128)))

    for col in range(4):
        a = fe[0:80, 128 * col:128 * (col + 1)].astype(F32)
        b = fe[80:160, 128 * col:128 * (col + 1)].astype(F32)
        fsrc[2 * col] = (a * half[0] + pltpu.roll(b, 64, 1) * half[1]).astype(BF)
        fsrc[2 * col + 1] = (pltpu.roll(a, 64, 1) * half[0] + b * half[1]).astype(BF)
    chip = 4 * z + y
    fbuf[me] = fsrc[chip]
    u1[2 * z + c] = up[2 * c + z]
    cbuf[me] = ci[...]
    pl.semaphore_wait(barrier_sem, len(peers))

    steps = [(0, 1), (0, 3), (1, 0), (0, 2), (1, 1), (1, 3), (1, 2)]
    for dz, dy in steps:
        zz, yy = (z + dz) % 2, (y + dy) % 4
        send(("f", dz, dy), fsrc.at[4 * zz + yy], fbuf.at[me], "shard", sid(zz, yy, c))
    send("fp", fbuf.at[me], fbuf.at[me], "shard", pair)
    send("w", w.at[:, :, pl.ds(pl.multiple_of(256 * (1 - c), 256), 256)], w2s.at[:, c], "shard", pair)
    w2s[:, c] = w[:, :, pl.ds(pl.multiple_of(256 * c, 256), 256)]

    def relay(dz, dy):
        frm = sid((z + dz) % 2, (y + 4 - dy) % 4, c)
        got(("f", dz, dy), fbuf.at[frm])
        send(("fr", dz, dy), fbuf.at[frm], fbuf.at[frm], "shard", pair)

    relay(0, 1)
    relay(0, 3)
    got("w", w2s.at[:, 1 - c])
    for dt in range(3):
        wts[dt] = jnp.transpose(w2s[9 * dt:9 * dt + 9].reshape(576, 256).astype(F32)).astype(BF)
    for dz, dy in steps[2:]:
        relay(dz, dy)
    got("fp", fbuf.at[pair])
    trio = [(0, 1), (1, 0), (1, 1)]
    for dz, dc in trio:
        zz, cc = (z + dz) % 2, (c + dc) % 2
        send(("u1", dz, dc), up.at[2 * cc + zz], u1.at[2 * z + c], "shard", sid(zz, y, cc))
    for d in range(1, NS):
        send(("b", d), ci, cbuf.at[me], "shard", (me + d) % NS)
    for dz, dy in steps:
        got(("fr", dz, dy), fbuf.at[sid((z + dz) % 2, (y + 4 - dy) % 4, 1 - c)])

    sel64, sel32 = picks(64, 64), picks(32, 32)

    def features(t):
        pieces = []
        for h in range(2):
            p = 32 * t + 16 * h
            k = p // 80
            p = p - 80 * k
            pieces.append(fbuf[:, p:p + 16, :] * halfb[k][None])
        rows = jnp.concatenate(pieces, axis=1).reshape(LP, 128)
        f = dot_nt(sel64, rows)
        for dw in range(3):
            fc = col_shift(f, dw - 1, m)
            for dr in range(3):
                k = 3 * dr + dw
                pat[t, 64 * k:64 * (k + 1), :] = row_shift(fc, dr - 1, m).astype(BF)

    def comp(t):
        features(t)
        acc = None
        for dt in range(3):
            if t - 2 + dt >= 0:
                d = dot(wts[dt], pat[t - 2 + dt])
                acc = d if acc is None else acc + d
        for k in range(8):
            part[k // 4, k % 4, t] = acc[32 * k:32 * (k + 1)].astype(BF)
        if t in SCATTER_DIRECT:
            send(("s1a", t), part.at[:, far, t], rxf.at[t], "shard", far_id)
            send(("s2a", t), part.at[:, yp, t], rx2.at[0, t], "shard", up_id)
            send(("s2b", t), part.at[:, ym, t], rx2.at[1, t], "shard", down_id)
            return
        send(("s1a", t), part.at[:, far, t, pl.ds(0, 16)], rx1.at[0, t], "shard", up_id)
        send(("s1b", t), part.at[:, far, t, pl.ds(16, 16)], rx1.at[1, t], "shard", down_id)

    def s2(t):
        if t in SCATTER_DIRECT:
            return
        got(("s1a", t), rx1.at[0, t])
        tx2[0, t, :, 0:16] = (part[:, yp, t, 0:16].astype(F32) + rx1[0, t].astype(F32)).astype(BF)
        tx2[0, t, :, 16:32] = part[:, yp, t, 16:32]
        send(("s2a", t), tx2.at[0, t], rx2.at[0, t], "shard", up_id)
        got(("s1b", t), rx1.at[1, t])
        tx2[1, t, :, 16:32] = (part[:, ym, t, 16:32].astype(F32) + rx1[1, t].astype(F32)).astype(BF)
        tx2[1, t, :, 0:16] = part[:, ym, t, 0:16]
        send(("s2b", t), tx2.at[1, t], rx2.at[1, t], "shard", down_id)

    def s3(t):
        got(("s2a", t), rx2.at[0, t])
        got(("s2b", t), rx2.at[1, t])
        give = part[o, y, t].astype(F32) + rx2[0, t, o].astype(F32) + rx2[1, t, o].astype(F32)
        if t in SCATTER_DIRECT:
            got(("s1a", t), rxf.at[t])
            give = give + rxf[t, o].astype(F32)
        txz[t] = give.astype(BF)
        send(("s3", t), txz.at[t], rxz.at[t], "shard", over)
        keep = part[z, y, t].astype(F32) + rx2[0, t, z].astype(F32) + rx2[1, t, z].astype(F32)
        if t in SCATTER_DIRECT:
            keep = keep + rxf[t, z].astype(F32)
        conv[t] = keep

    def s4(t):
        got(("s3", t), rxz.at[t])
        conv[t] = conv[t] + rxz[t].astype(F32)

    def u_second():
        for dz, dc in trio:
            zz, cc = (z + dz) % 2, (c + dc) % 2
            got(("u1", dz, dc), u1.at[2 * zz + cc])
        for q in range(4):
            acc = None
            for g in range(4):
                v = u1[g].astype(F32)
                v = v if g == q else pltpu.roll(v, (32 * (g - q)) % 128, 1)
                acc = v * grp[g] if acc is None else acc + v * grp[g]
            u2s[q] = acc.astype(BF)
        for dy in (1, 3, 2):
            yy = (y + dy) % 4
            send(("u2", dy), u2s.at[yy], u2.at[y], "shard", sid(z, yy, c))
        u2[y] = u2s[y]

    def u_third():
        for dy in (1, 3, 2):
            got(("u2", dy), u2.at[(y + 4 - dy) % 4])
        for t in range(T):
            blocks = []
            for s in range(NS):
                blocks.append(u2[(s // 2) % 4, 32 * t:32 * t + 32, :] * grpb[2 * (s // 8) + s % 2])
            ut[t] = dot_nt(sel32, jnp.concatenate(blocks, axis=0))

    def run(events):
        for _, _, f, args in sorted(events, key=lambda e: e[:2]):
            f(*args)

    ev = []
    for t in range(T):
        ev += [
            (1.5 * t, 0, comp, (t,)), (2.6 + 2.1 * t, 1, s2, (t,)),
            (5.2 + 2.1 * t, 2, s3, (t,)), (11.0 + 2.1 * t, 3, s4, (t,)),
        ]
    ev += [(9.0, 9, u_second, ()), (17.0, 9, u_third, ())]
    run(ev)

    count = length.astype(F32) * float(R * WD * NS * 16)
    s_one = jnp.zeros((32, LP), F32)
    s_two = jnp.zeros((32, LP), F32)
    for t in range(T):
        v = conv[t] * mk[t]
        s_one = s_one + v
        s_two = s_two + conv[t] * v
    mean = group_sum(s_one) / count
    inv = lax.rsqrt(group_sum(s_two) / count - mean * mean + EPS)
    mine32 = pl.ds(pl.multiple_of(32 * y, 32), 32)
    gain, bias = gcol[0, mine32, 0:1], gcol[1, mine32, 0:1]
    a1 = jnp.zeros((32, LP), F32)
    a2 = jnp.zeros((32, LP), F32)
    for t in range(T):
        n = (conv[t] - mean) * inv
        pre = n * gain + bias
        sg = jax.nn.sigmoid(pre)
        act[t] = pre * sg * mk[t]
        d = ut[t] * mk[t] * sg * (1.0 + pre * (1.0 - sg))
        a1 = a1 + d
        a2 = a2 + d * n
        nrm[t] = n
        dpr[t] = d
    bterm = jnp.sum(a1, axis=1, keepdims=True)
    gterm = jnp.sum(a2, axis=1, keepdims=True)
    t1 = group_sum(gain * bterm) / count
    t2 = group_sum(gain * gterm) / count

    lo, hi = pl.ds(0, 16), pl.ds(16, 16)
    order = [4, 3, 2, 1, 0]
    for t in order:
        own[t] = (inv * (dpr[t] * gain - t1 - nrm[t] * t2) * mk[t]).astype(BF)
        send(("g0", t), own.at[t], dcs.at[z, y, t], "shard", over)
        send(("g1", t), own.at[t], dcs.at[z, y, t], "shard", up_id)
        send(("g2", t), own.at[t], dcs.at[z, y, t], "shard", down_id)
        if t in GATHER_DIRECT:
            send(("g3", t), own.at[t], dcs.at[z, y, t], "shard", far_id)
    for t in order:
        dcs[z, y, t] = own[t]

    def first_out(kind, get, t0, t1):
        pack_out(kind, get, t0, t1)
        send_out(kind, t0, t1)

    def pack_out(kind, get, t0, t1):
        for t in range(t0, t1):
            v = get(t)
            nat = jnp.transpose(jnp.concatenate([v, v, v, v], axis=0))
            for q in range(4):
                acc = None
                for g in range(4):
                    r0 = 32 * sid(g // 2, q, g % 2)
                    piece = nat[r0:r0 + 32] * grp[g]
                    acc = piece if acc is None else acc + piece
                d1s[kind, q, 32 * t:32 * t + 32, :] = acc.astype(BF)

    def send_out(kind, t0, t1):
        for dy in (1, 3, 2):
            yy = (y + dy) % 4
            part_of = pl.ds(32 * t0, 32 * (t1 - t0))
            send(
                ("d1", kind, t0, dy), d1s.at[kind, yy, part_of], d1.at[kind, y, part_of], "shard", sid(z, yy, c)
            )
        d1[kind, y, 32 * t0:32 * t1] = d1s[kind, y, 32 * t0:32 * t1]

    def second_out(kind, dst, t0, t1):
        part_of = pl.ds(32 * t0, 32 * (t1 - t0))
        for dy in (1, 3, 2):
            got(("d1", kind, t0, dy), d1.at[kind, (y + 4 - dy) % 4, part_of])
        for g in range(4):
            acc = None
            for q in range(4):
                v = d1[kind, q, 32 * t0:32 * t1].astype(F32)
                v = v if g == q else pltpu.roll(v, (32 * (q - g)) % 128, 1)
                acc = v * grp[q] if acc is None else acc + v * grp[q]
            d2s[kind, g, 32 * t0:32 * t1] = acc.astype(BF)
        for dz, dc in trio:
            zz, cc = (z + dz) % 2, (c + dc) % 2
            send(
                ("d2", kind, t0, dz, dc), d2s.at[kind, 2 * zz + cc, part_of], dst.at[2 * z + c, part_of],
                "shard", sid(zz, y, cc),
            )
        dst[2 * z + c, 32 * t0:32 * t1] = d2s[kind, 2 * z + c, 32 * t0:32 * t1]

    def third_out(kind, dst, t0, t1):
        part_of = pl.ds(32 * t0, 32 * (t1 - t0))
        for dz, dc in trio:
            got(("d2", kind, t0, dz, dc), dst.at[2 * ((z + dz) % 2) + (c + dc) % 2, part_of])

    def g_near(t):
        if t in GATHER_DIRECT:
            return
        got(("g1", t), dcs.at[z, ym, t])
        send(("g3", t), dcs.at[z, ym, t, lo], dcs.at[z, ym, t, lo], "shard", up_id)
        got(("g2", t), dcs.at[z, yp, t])
        send(("g4", t), dcs.at[z, yp, t, hi], dcs.at[z, yp, t, hi], "shard", down_id)

    def g_over(t):
        got(("g0", t), dcs.at[o, y, t])
        send(("g5", t), dcs.at[o, y, t], dcs.at[o, y, t], "shard", up_id)
        send(("g6", t), dcs.at[o, y, t], dcs.at[o, y, t], "shard", down_id)
        if t in GATHER_DIRECT:
            send(("g7", t), dcs.at[o, y, t], dcs.at[o, y, t], "shard", far_id)

    def g_far(t):
        if t in GATHER_DIRECT:
            return
        got(("g5", t), dcs.at[o, ym, t])
        send(("g7", t), dcs.at[o, ym, t, lo], dcs.at[o, ym, t, lo], "shard", up_id)
        got(("g6", t), dcs.at[o, yp, t])
        send(("g8", t), dcs.at[o, yp, t, hi], dcs.at[o, yp, t, hi], "shard", down_id)

    def g_done(t):
        if t in GATHER_DIRECT:
            got(("g1", t), dcs.at[z, ym, t])
            got(("g2", t), dcs.at[z, yp, t])
            got(("g3", t), dcs.at[z, far, t])
            got(("g5", t), dcs.at[o, ym, t])
            got(("g6", t), dcs.at[o, yp, t])
            got(("g7", t), dcs.at[o, far, t])
            return
        got(("g3", t), dcs.at[z, far, t, lo])
        got(("g4", t), dcs.at[z, far, t, hi])
        got(("g7", t), dcs.at[o, far, t, lo])
        got(("g8", t), dcs.at[o, far, t, hi])

    def dgrad(t):
        acc = None
        for dt in range(3):
            if t + 2 - dt < T:
                d = dot(w2s[9 * dt:9 * dt + 9].reshape(576, 256), dcs[:, :, t + 2 - dt].reshape(256, LP))
                acc = d if acc is None else acc + d
        total = None
        for dw in range(3):
            rows = None
            for dr in range(3):
                k = 3 * dr + dw
                s = row_shift(acc[64 * k:64 * (k + 1)], 1 - dr, m)
                rows = s if rows is None else rows + s
            s = col_shift(rows, 1 - dw, m)
            total = s if total is None else total + s
        for h in range(2):
            df[h, t] = total[32 * h:32 * (h + 1)]
            db[h, t] = total[32 * h:32 * (h + 1)].astype(BF)
        send(("pair", t), db.at[1 - c, t], drx.at[t], "shard", pair)

    def wgrad(t):
        dct = dcs[:, :, t].reshape(256, LP)
        for dt in range(3):
            if t - 2 + dt < 0:
                continue
            v = dot_nt(pat[t - 2 + dt], dct)
            if t < T - 1:
                v = v + wacc[dt]
            if t == 2 - dt:
                for k in range(9):
                    tap = 9 * dt + k
                    cw[tap // 4, tap % 4] = v[64 * k:64 * (k + 1)].astype(BF).reshape(4, 16, 256)
            else:
                wacc[dt] = v

    def dsum(t):
        got(("pair", t), drx.at[t])
        dft[t] = (df[c, t] + drx[t].astype(F32)).astype(BF).astype(F32) * mk[t]

    lo4, hi4 = pl.ds(0, 2), pl.ds(2, 2)

    xfar = xf * 4 + l

    def r1(g):
        if g in DIRECT:
            send(("r15", g), cw.at[g, xf], qx2.at[2, g], "dp", xfar)
            send(("r2", g), cw.at[g, xp], qx2.at[0, g], "dp", fwd)
            send(("r3", g), cw.at[g, xm], qx2.at[1, g], "dp", bwd)
            return
        send(("r0", g), cw.at[g, xf, lo4], qx1.at[0, g], "dp", fwd)
        send(("r1", g), cw.at[g, xf, hi4], qx1.at[1, g], "dp", bwd)

    def r2(g):
        if g in DIRECT:
            return
        got(("r0", g), qx1.at[0, g])
        qt2[0, g, 0:2] = (cw[g, xp, 0:2].astype(F32) + qx1[0, g].astype(F32)).astype(BF)
        qt2[0, g, 2:4] = cw[g, xp, 2:4]
        send(("r2", g), qt2.at[0, g], qx2.at[0, g], "dp", fwd)
        got(("r1", g), qx1.at[1, g])
        qt2[1, g, 2:4] = (cw[g, xm, 2:4].astype(F32) + qx1[1, g].astype(F32)).astype(BF)
        qt2[1, g, 0:2] = cw[g, xm, 0:2]
        send(("r3", g), qt2.at[1, g], qx2.at[1, g], "dp", bwd)

    def r3(g):
        got(("r2", g), qx2.at[0, g])
        got(("r3", g), qx2.at[1, g])
        tot = cw[g, x].astype(F32) + qx2[0, g].astype(F32) + qx2[1, g].astype(F32)
        if g in DIRECT:
            got(("r15", g), qx2.at[2, g])
            tot = tot + qx2[2, g].astype(F32)
        sx[g] = tot.astype(BF)
        for k in (3, 2, 1):
            send(("r4", k, g), sx.at[g, (l + k) % 4], rz.at[g, k], "dp", x * 4 + (l + k) % 4)

    def r4(g):
        tot = sx[g, l].astype(F32)
        for k in (1, 2, 3):
            got(("r4", k, g), rz.at[g, k])
            tot = tot + rz[g, k].astype(F32)
        out[g, x, l] = tot.astype(BF)
        for k in (3, 2, 1):
            send(("r7", k, g), out.at[g, x, l], out.at[g, x, l], "dp", x * 4 + (l + k) % 4)

    def r5(g):
        for k in (1, 2, 3):
            got(("r7", k, g), out.at[g, x, (l + 4 - k) % 4])
        send(("r10", g), out.at[g, x], out.at[g, x], "dp", fwd)
        send(("r11", g), out.at[g, x], out.at[g, x], "dp", bwd)
        if g in DIRECT:
            send(("r16", g), out.at[g, x], out.at[g, x], "dp", xfar)

    def r6(g):
        if g in DIRECT:
            return
        got(("r10", g), out.at[g, xm])
        send(("r12", g), out.at[g, xm, lo4], out.at[g, xm, lo4], "dp", fwd)
        got(("r11", g), out.at[g, xp])
        send(("r13", g), out.at[g, xp, hi4], out.at[g, xp, hi4], "dp", bwd)

    mine = pl.ds(pl.multiple_of(256 * c, 256), 256)
    other = pl.ds(pl.multiple_of(256 * (1 - c), 256), 256)

    def r7(g):
        if g in DIRECT:
            got(("r10", g), out.at[g, xm])
            got(("r11", g), out.at[g, xp])
            got(("r16", g), out.at[g, xf])
        else:
            got(("r12", g), out.at[g, xf, lo4])
            got(("r13", g), out.at[g, xf, hi4])
        send(("r14", g), out.at[g, :, pl.ds(2 * (1 - c), 2)], fin.at[g, :, :, :, mine], "shard", pair)
        fin[g, :, :, :, mine] = out[g, :, pl.ds(2 * c, 2)]

    def m1():
        for d in range(1, NS):
            got(("b", d), cbuf.at[(me + NS - d) % NS])
        grpi = [(lane // 32 == g).astype(jnp.int32) for g in range(4)]
        bit32 = lax.broadcasted_iota(jnp.int32, (32, LP), 0)
        acc = jnp.zeros((32, 128), F32)
        for f in range(4):
            cols = []
            for q in range(4):
                v = None
                for j in range(4):
                    r = cbuf[4 * q + j]
                    r = r if j == f else pltpu.roll(r, (32 * (j - f)) % 128, 1)
                    v = r * grpi[j] if v is None else v + r * grpi[j]
                cols.append(v)
            for t in ((0, 4) if f == 0 else (f,)):
                code = jnp.concatenate([v[t // 4:t // 4 + 1] for v in cols], axis=1)
                code = jnp.broadcast_to(code, (32, LP))
                signs = jnp.where(bit32 < CODE_BITS, (lax.shift_right_logical(code, bit32) & 1) * 2 - 1, 0)
                rhs = jnp.concatenate([dft[t], jnp.zeros((96, LP), F32)], axis=0).astype(BF)
                acc = acc + dot_nt(signs.astype(F32).astype(BF), rhs)
        cols = jnp.where(lane == 0, gterm, jnp.where(lane == 1, bterm, 0.0))
        gb = jnp.transpose(jnp.concatenate([cols, jnp.zeros((96, 128), F32)], axis=0))
        e = acc[16:24] + pltpu.roll(gb[0:8], 2, 0)
        sm[...] = acc[0:8] + pltpu.roll(acc[8:16], 32, 1) + pltpu.roll(e, 64, 1)
        xb[x] = sm[...]
        for k in (2, 1, 3):
            send(("m1", k), sm, xb.at[x], "dp", ((x + k) % 4) * 4 + l)

    def m2():
        for k in (1, 2, 3):
            got(("m1", k), xb.at[(x + 4 - k) % 4])
        zb[l] = (xb[0] + xb[1]) + (xb[2] + xb[3])
        for k in (3, 2, 1):
            send(("m2", k), zb.at[l], zb.at[l], "dp", x * 4 + (l + k) % 4)

    def m3():
        for k in (1, 2, 3):
            got(("m2", k), zb.at[(l + 4 - k) % 4])
        smo[me] = (zb[0] + zb[1]) + (zb[2] + zb[3])
        for d in range(1, NS):
            send(("m3", d), smo.at[me], smo.at[me], "shard", (me + d) % NS)

    def m4():
        for d in range(1, NS):
            got(("m3", d), smo.at[(me + NS - d) % NS])

    ev = [(2.0 + 0.5 * t, 0, pack_out, (0, lambda t: act[t], t, t + 1)) for t in range(T)]
    ev += [(9.6, 0, send_out, (0, 0, T)), (24.2, 0, second_out, (0, dec, 0, T))]
    for i, t in enumerate(order):
        ev += [
            (2.4 + 1.1 * i, 1, g_near, (t,)), (4.5 + 1.2 * i, 2, g_over, (t,)),
            (8.5 + 1.6 * i, 3, g_far, (t,)), (11.0 + 2.1 * i, 4, g_done, (t,)),
            (11.0 + 2.1 * i, 5, wgrad, (t,)), (11.1 + 2.1 * i, 30, dgrad, (t,)),
            (13.2 + 2.1 * i, 7, dsum, (t,)),
        ]
    ready = (15.22, 15.24, 17.32, 17.34, 19.42, 19.44, 19.46)
    for g in range(G):
        at = ready[g]
        lag = max(0.0, 15.3 + LAG * g - at)
        offs = OFF_D if g in DIRECT else OFF_R
        for off, n, f in zip(offs, range(20, 27), (r1, r2, r3, r4, r5, r6, r7)):
            ev.append((at + off + (lag if off else 0.0), n, f, (g,)))
    get = lambda t: dft[t]
    ev += [
        (TAIL[0], 30, first_out, (1, get, 2, T)), (TAIL[1], 31, second_out, (1, gho, 2, T)),
        (TAIL[2], 40, first_out, (1, get, 0, 2)), (TAIL[3], 41, m1, ()),
        (TAIL[4], 41, second_out, (1, gho, 0, 2)), (TAIL[5], 42, m2, ()), (TAIL[6], 43, m3, ()),
        (37.0, 45, m4, ()), (37.1, 46, third_out, (0, dec, 0, T)),
        (37.2, 47, third_out, (1, gho, 2, T)), (37.3, 48, third_out, (1, gho, 0, 2)),
    ]
    cw[6, 3] = jnp.zeros((4, 16, 256), BF)
    run(ev)
    for g in range(G):
        got(("r14", g), fin.at[g, :, :, :, other])
    wires.finish()


def block(lengths, codes, hid, emb, w, gain, bias, cot):
    v = pltpu.VMEM
    piece = (16, 256)
    return pl.pallas_call(
        block_body,
        out_shape=(
            jax.ShapeDtypeStruct((4, 160, 128), BF),
            jax.ShapeDtypeStruct((4, 160, 128), BF),
            jax.ShapeDtypeStruct((G, 4, 2, 16, 512), BF),
            jax.ShapeDtypeStruct((NS, 8, 128), F32),
        ),
        in_specs=[pl.BlockSpec(memory_space=pltpu.SMEM)] + [VM] * 7, out_specs=(VM,) * 4,
        scratch_shapes=[
            v((8, 128), jnp.int32),
            v((128, 512), BF), v((160, 512), BF), v((4, 160, 128), BF), v((2, 128, 128), F32),
            v((NS, 8, 128), jnp.int32),
            v((8, 80, 128), BF), v((NS, 80, 128), BF),
            v((4, 160, 128), BF), v((4, 160, 128), BF), v((4, 160, 128), BF),
            v((27, 2, 32, 256), BF), v((3, 256, 576), BF),
            v((T, 576, LP), BF), v((2, 4, T, 32, LP), BF),
            v((2, T, 2, 16, LP), BF), v((2, T, 2, 32, LP), BF), v((2, T, 2, 32, LP), BF),
            v((T, 2, 32, LP), BF),
            v((T, 32, LP), BF), v((T, 32, LP), BF), v((T, 32, LP), F32),
            v((T, 32, LP), F32), v((T, 32, LP), F32), v((T, 32, LP), F32), v((T, 32, LP), F32),
            v((T, 32, LP), BF), v((2, 4, T, 32, LP), BF), v((3, 576, 256), F32),
            v((G, 4, 4) + piece, BF),
            v((2, T, 32, LP), F32), v((2, T, 32, LP), BF), v((T, 32, LP), BF), v((T, 32, LP), F32),
            v((2, 4, 160, 128), BF), v((2, 4, 160, 128), BF), v((2, 4, 160, 128), BF),
            v((G, 4, 4) + piece, BF), v((2, G, 2) + piece, BF), v((2, G, 4) + piece, BF),
            v((3, G, 4) + piece, BF), v((G, 4) + piece, BF), v((G, 4) + piece, BF),
            v((8, 128), F32), v((4, 8, 128), F32), v((4, 8, 128), F32),
            pltpu.SemaphoreType.DMA((N_WIRES,)), pltpu.SemaphoreType.DMA((N_WIRES,)),
        ],
        compiler_params=params(0), name="block",
    )(lengths, codes, hid, emb, w, gain, bias, cot)


def outputs_body(dec, gho, fin, smo, dec_o, gh_o, gc_o, ge_o, gg_o, gb_o):
    lane = lax.broadcasted_iota(jnp.int32, (1, 128), 1)
    grp = [(lane // 32 == g).astype(F32) for g in range(4)]

    def gathered(parts):
        acc = None
        for g, (v, q) in enumerate(parts):
            v = v.astype(F32)
            v = v if g == q else pltpu.roll(v, (32 * (g - q)) % 128, 1)
            acc = v * grp[g] if acc is None else acc + v * grp[g]
        return acc

    for tap in range(27):
        gc_o[tap] = fin[tap // 4, tap % 4].reshape(32, 512).astype(F32)
    back = placing(1)
    for t in range(T):
        rows = slice(32 * t, 32 * t + 32)
        v = jnp.concatenate([dec[0, rows], dec[2, rows], dec[1, rows], dec[3, rows]], axis=0)
        dec_o[128 * t:128 * t + 128] = dot(back, v).astype(BF)
    for zz in range(2):
        for h in range(2):
            col = 2 * zz + h
            v = gathered([(gho[2 * zz + g % 2], 2 * h + g // 2) for g in range(4)])
            gh_o[:, :, :, 128 * col:128 * (col + 1)] = v.reshape(T, R, WD, 128).astype(BF)
    for q in range(4):
        cols = slice(128 * q, 128 * (q + 1))
        for a in range(3):
            v = gathered([(smo[4 * q + j], a) for j in range(4)])
            n = min(8, CODE_BITS - 8 * a)
            ge_o[8 * a:8 * a + n, cols] = v[0:n]
        v = gathered([(smo[sid(q % 2, j, q // 2)], 2) for j in range(4)])
        gg_o[q:q + 1] = v[2:3]
        gb_o[q:q + 1] = v[3:4]


def outputs(dec, gho, fin, smo):
    s = jax.ShapeDtypeStruct
    return pl.pallas_call(
        outputs_body,
        out_shape=(
            s((640, 128), BF), s((T, R, WD, 512), BF), s((27, 32, 512), F32), s((CODE_BITS, 512), F32),
            s((4, 128), F32), s((4, 128), F32),
        ),
        in_specs=[VM] * 4, out_specs=(VM,) * 6, compiler_params=params(), name="outputs",
    )(dec, gho, fin, smo)


def on_device(codes, lengths, hidden, embed, conv_weight, gain, bias, cotangent):
    raw = block(
        lengths, codes[0].transpose(0, 2, 1), hidden[0], embed, conv_weight.transpose(1, 0, 2),
        gain.reshape(4, 128), bias.reshape(4, 128), cotangent.reshape(640, 128),
    )
    dec, gh, gc, ge, gg, gb = outputs(*raw)
    return (
        dec.reshape(1, T, 2 * R, 2 * WD, 128), gh[None], gc.transpose(1, 0, 2), ge,
        gg.reshape(512), gb.reshape(512),
    )


def solution(mesh):
    return jax.shard_map(
        on_device,
        mesh=mesh,
        in_specs=(
            P("dp", None, None, "shard"),
            P("dp"),
            P("dp", None, None, "shard", None),
            P(),
            P("shard", None, None),
            P(),
            P(),
            P("dp", None, None, "shard", None),
        ),
        out_specs=(
            P("dp", None, None, "shard", None),
            P("dp", None, None, "shard", None),
            P("shard", None, None),
            P(),
            P(),
            P(),
        ),
        check_vma=False,
    )
```
